32 devices in a mesh: group: 4 (over x, core), member: 8 (over z, y).
Axes of the slice: x: 2, y: 2, z: 4, core: 2. Of those that a mesh axis runs over, the one named last changes fastest.
Arguments:
- queries: bfloat16 [32, 32, 128], P(('group', 'member')), may hold values from -1.2 to 1.2
- pages: bfloat16 [192, 1024, 128], P(('group', 'member')), may hold values from -1.2 to 1.2
- users: int32 [192, 32], P(('group', 'member')), may hold values from 0 to 31, as said below
- page_count: int32 [192], P(('group', 'member')), may hold values from 1 to 32
- teacher: float32 [192, 32], P(('group', 'member')), may hold values from 4 to 12
Outputs:
- scores: float32 [192, 32], P(('group', 'member'))
- query_grad: float32 [32, 32, 128], P(('group', 'member'))
- page_grad: bfloat16 [192, 1024, 128], P(('group', 'member'))
The draws below stay inside these ranges and needn't reach their ends.
Inputs may be any that keep to these rules, and one draw needn't show every extreme that they name: `users`: slots at or past page_count hold valid ids that are ignored. Queries are numbered in the order of their owning devices. Over the slots of the pages of one device, exactly 8 distinct queries of each group (of 8 consecutive query ids) appear, counting dead slots too.
All inputs are finite; a program needn't handle non-finite values.
Results may differ from the reference program's by a relative error of at most 0.014.
Values may be sent and summed in bfloat16 or wider, within the bound.
No kernel may reach another device: no remote copies, remote signals or barrier semaphores. Data moves between devices by JAX's collectives and lax.ppermute only.
A program may use at most 64 MiB of HBM per device.

```python
import jax
import jax.numpy as jnp
from jax import lax

DIM = 128
QTOK = 32
PTOK = 1024
USE = 32
CAP = 8
Q_DEV = 1
PG_DEV = 6
QUERIES = 32
PAGES = 192
N_GROUP = 4
N_MEMBER = 8
DEVICES = 32


def draw_pages(key, part):
    noise_key = jax.random.fold_in(key, 11)
    values = jnp.clip(0.1 * jax.random.normal(noise_key, (PAGES, PTOK, DIM), jnp.float32), -0.6, 0.6)
    return values.astype(jnp.bfloat16)


def draw_queries(key, part):
    noise_key = jax.random.fold_in(key, 13)
    values = jnp.clip(0.1 * jax.random.normal(noise_key, (QUERIES, QTOK, DIM), jnp.float32), -0.6, 0.6)
    return values.astype(jnp.bfloat16)


def member_picks(member_key):
    return jax.random.permutation(member_key, N_MEMBER * Q_DEV)[:CAP]


def device_order(device_key):
    return jax.random.permutation(device_key, N_GROUP * CAP)


def slot_order(device_key):
    return jax.random.permutation(device_key, PG_DEV * USE)


def draw_users(key, part):
    group_rows = N_MEMBER * Q_DEV
    slot_total = PG_DEV * USE
    listed = N_GROUP * CAP
    pick_keys = jax.random.split(jax.random.fold_in(key, 21), DEVICES * N_GROUP)
    picks = jax.vmap(member_picks)(pick_keys).astype(jnp.int32).reshape(DEVICES, N_GROUP, CAP)
    offsets = (jnp.arange(N_GROUP, dtype=jnp.int32) * group_rows)[None, :, None]
    candidates = (picks + offsets).reshape(DEVICES, listed)
    first = jax.vmap(device_order)(jax.random.split(jax.random.fold_in(key, 22), DEVICES)).astype(jnp.int32)
    extra_one = jax.random.randint(jax.random.fold_in(key, 23), (DEVICES, slot_total - listed), 0, listed)
    extra_two = jax.random.randint(jax.random.fold_in(key, 24), (DEVICES, slot_total - listed), 0, listed)
    extra = jnp.minimum(extra_one, extra_two).astype(jnp.int32)
    chosen = jnp.concatenate([first, extra], axis=1)
    order = jax.vmap(slot_order)(jax.random.split(jax.random.fold_in(key, 25), DEVICES)).astype(jnp.int32)
    chosen = jnp.take_along_axis(chosen, order, axis=1)
    result = jnp.take_along_axis(candidates, chosen, axis=1)
    return result.reshape(PAGES, USE).astype(jnp.int32)


def touch_ends(drawn, rng, smallest, largest):
    longest = drawn.shape.index(max(drawn.shape))
    spots = []
    for shift in (0, 1):
        where = [jax.random.randint(jax.random.fold_in(rng, axis), (), 0, length) for axis, length in enumerate(drawn.shape)]
        where[longest] = (where[longest] + shift) % drawn.shape[longest]
        spots.append(tuple(where))
    return drawn.at[spots[0]].set(smallest).at[spots[1]].set(largest)


def shard_levels(stream_key, shape, cuts, least, high):
    loudness, own = 1.0, jax.random.fold_in(stream_key, 6)
    for position, blocks in cuts:
        heights = jnp.exp(jax.random.uniform(jax.random.fold_in(own, position), (blocks,), jnp.float32, least / len(cuts), high / len(cuts)))
        loudness = loudness * jnp.repeat(heights, shape[position] // blocks).reshape([-1 if axis == position else 1 for axis in range(len(shape))])
    return loudness


def setup_inputs(seed: int = 0) -> dict:
    key_list = jax.random.split(jax.random.key(seed), 6)
    return {
        "queries": draw_queries(jax.random.fold_in(key_list[5], 71), 0),
        "pages": draw_pages(jax.random.fold_in(key_list[5], 71), 0),
        "users": draw_users(jax.random.fold_in(key_list[5], 71), 0),
        "page_count": touch_ends(jax.random.randint(key_list[3], (PAGES,), 1, USE + 1), jax.random.fold_in(key_list[3], 1), 1, USE).astype(jnp.int32),
        "teacher": jnp.clip(4.0 + 8.0 * jax.random.uniform(key_list[4], (PAGES, USE), jnp.float32) ** shard_levels(key_list[4], (PAGES, USE), ((0, 32),), -0.2, 0.2), 4.0, 12.0),
    }


normalized_exponent_divisor = 0.05


def reference(queries, pages, users, page_count, teacher):
    query_f32 = queries.astype(jnp.float32)
    slot_ids = jnp.arange(USE).astype(jnp.int32)

    def page_step(grad_total, inputs):
        page_tile, user_row, active_total, teacher_row = inputs
        document_single_float = page_tile.astype(jnp.float32)
        chosen = query_f32[user_row]
        cosine_affinity = jnp.einsum("uqd,pd->uqp", chosen, document_single_float)
        pairing_coefficients = jax.nn.softmax(cosine_affinity / normalized_exponent_divisor, axis=-1)
        aligned_rating = jnp.sum(pairing_coefficients * cosine_affinity, axis=-1)
        score = jnp.sum(aligned_rating, axis=-1)
        live = slot_ids < active_total
        unaligned_rating = jnp.where(live, score - teacher_row, jnp.zeros_like(score))
        rating_gradient_factor = unaligned_rating[:, None, None] * pairing_coefficients * (1.0 + (cosine_affinity - aligned_rating[:, :, None]) / normalized_exponent_divisor)
        rating_gradient_factor = lax.optimization_barrier(rating_gradient_factor.astype(jnp.bfloat16)).astype(jnp.float32)
        query_part = jnp.einsum("uqp,pd->uqd", rating_gradient_factor, document_single_float)
        page_part = jnp.einsum("uqp,uqd->pd", rating_gradient_factor, chosen)
        grad_total = grad_total.at[user_row].add(query_part)
        return grad_total, (jnp.where(live, score, jnp.zeros_like(score)), page_part.astype(jnp.bfloat16))

    initial = jnp.zeros(queries.shape, jnp.float32)
    query_grad, (scores, page_grad) = lax.scan(page_step, initial, (pages, users, page_count, teacher))
    return scores, query_grad, page_grad
```

```python
import functools

import jax
import jax.numpy as jnp
from jax import lax
from jax.experimental import pallas as pl
from jax.experimental.pallas import tpu as pltpu
from jax.sharding import PartitionSpec as P

AXES = ("group", "member")
BLOCK = 8
INV_TEMP = 20.0
LOG2E = 1.4426950408889634


def grad_kernel(order, blocks, q_ref, page_ref, page_t_ref, cnt_ref, sum_ref, diag_ref,
                dq_ref, slope_ref, score_ref, qb, sim, wts, acc):
    n_pages, p_tok, dim = page_ref.shape
    n_tok = q_ref.shape[1]
    width = BLOCK * n_tok
    per_page = slope_ref.shape[0] // n_pages
    acc[...] = jnp.zeros_like(acc)
    chunk = 64
    parts = [pl.ds(r, chunk) for r in range(0, p_tok, chunk)]

    def fold(x, op):
        x = x.reshape(chunk // 8, 8, width)
        out = x[0]
        for i in range(1, chunk // 8):
            out = op(out, x[i])
        return out

    def block_step(p, j):
        b = p * per_page + j
        for k in range(BLOCK):
            qb[pl.ds(k * n_tok, n_tok), :] = q_ref[order[p, j * BLOCK + k]]
        sim[...] = lax.dot_general(
            page_ref[p], qb[...], (((1,), (1,)), ((), ())), preferred_element_type=jnp.float32
        )
        top = fold(sim[parts[0], :], jnp.maximum)
        for r in parts[1:]:
            top = jnp.maximum(top, fold(sim[r, :], jnp.maximum))
        top = jnp.max(top, axis=0, keepdims=True)
        total = jnp.zeros((8, width), jnp.float32)
        mass = jnp.zeros((8, width), jnp.float32)
        for r in parts:
            s = sim[r, :]
            e = jnp.exp2((s - top) * (INV_TEMP * LOG2E))
            wts[r, :] = e
            total += fold(e, jnp.add)
            mass += fold(e * s, jnp.add)
        inv = 1.0 / jnp.sum(total, axis=0, keepdims=True)
        matched = jnp.sum(mass, axis=0, keepdims=True) * inv
        hi = matched.astype(jnp.bfloat16)
        rest = matched - hi.astype(jnp.float32)
        mid = rest.astype(jnp.bfloat16)
        low = (rest - mid.astype(jnp.float32)).astype(jnp.bfloat16)
        pieces = jnp.concatenate([hi, mid, low], axis=0)
        score = jnp.sum(
            jnp.dot(pieces, diag_ref[...], preferred_element_type=jnp.float32),
            axis=0, keepdims=True)
        score_ref[b] = score
        mismatch = cnt_ref[b] * score - sum_ref[b]
        scale = mismatch * inv
        beta = scale * INV_TEMP
        alpha = scale - beta * matched
        for r in parts:
            slope_ref[b, r, :] = (wts[r, :] * (alpha + beta * sim[r, :])).astype(jnp.bfloat16)
        part_t = jnp.dot(page_t_ref[p], slope_ref[b], preferred_element_type=jnp.float32)
        part = part_t.T
        for k in range(BLOCK):
            acc[order[p, j * BLOCK + k]] += part[k * n_tok:(k + 1) * n_tok, :]

    def page_step(p, carry):
        def inner(j, c):
            block_step(p, j)
            return c
        return lax.fori_loop(0, blocks[p], inner, carry)

    lax.fori_loop(0, n_pages, page_step, 0)
    dq_ref[...] = acc[...].astype(dq_ref.dtype)


def page_kernel(order, blocks, q_ref, slope_ref, out_ref, qb):
    n_pages, p_tok, dim = out_ref.shape
    n_tok = q_ref.shape[1]
    width = BLOCK * n_tok
    per_page = slope_ref.shape[0] // n_pages
    for p in range(n_pages):
        for k in range(per_page * BLOCK):
            qb[pl.ds(k * n_tok, n_tok), :] = q_ref[order[p, k]]
        for n in range(1, per_page + 1):
            @pl.when(blocks[p] == n)
            def _():
                total = jnp.dot(slope_ref[p * per_page], qb[pl.ds(0, width), :],
                                preferred_element_type=jnp.float32)
                for j in range(1, n):
                    total += jnp.dot(slope_ref[p * per_page + j], qb[pl.ds(j * width, width), :],
                                     preferred_element_type=jnp.float32)
                out_ref[p] = total.astype(out_ref.dtype)


def body(queries, pages, users, page_count, teacher):
    n_dev = lax.axis_size("group") * lax.axis_size("member")
    own, n_tok, dim = queries.shape
    n_pages, p_tok, _ = pages.shape
    slots = users.shape[1]
    n_query = n_dev * own
    per_page = slots // BLOCK
    n_blocks = n_pages * per_page
    width = BLOCK * n_tok

    copies = jnp.broadcast_to(queries[None], (n_dev, own, n_tok, dim))
    gathered = lax.all_to_all(copies, AXES, split_axis=0, concat_axis=0, tiled=True)
    gathered = gathered.reshape(n_query, n_tok, dim)

    slot_ids = lax.iota(jnp.int32, slots)
    live = slot_ids[None, :] < page_count[:, None]
    same = (users[:, :, None] == users[:, None, :]) & live[:, :, None] & live[:, None, :]
    earlier = slot_ids[None, :] < slot_ids[:, None]
    first = live & ~jnp.any(same & earlier[None], axis=2)
    rank = jnp.sum(jnp.where(first[:, None, :] & earlier[None], 1, 0), axis=2)
    put = first[:, :, None] & (rank[:, :, None] == slot_ids[None, None, :])
    order = jnp.sum(jnp.where(put, users[:, :, None], 0), axis=1)
    number = jnp.sum(first.astype(jnp.int32), axis=1)
    blocks = (number + BLOCK - 1) // BLOCK
    hits = jnp.sum(same.astype(jnp.float32), axis=2)
    aims = jnp.sum(jnp.where(same, teacher[:, None, :], 0.0), axis=2)
    cnt = jnp.sum(jnp.where(put, hits[:, :, None], 0.0), axis=1)
    aim = jnp.sum(jnp.where(put, aims[:, :, None], 0.0), axis=1)
    place = jnp.sum(jnp.where(same & first[:, None, :], rank[:, None, :], 0), axis=2)

    def lanes(x):
        return jnp.repeat(x.reshape(n_blocks, 1, BLOCK), n_tok, axis=2)

    lane = lax.iota(jnp.int32, width) // n_tok
    diag = (lane[:, None] == lane[None, :]).astype(jnp.bfloat16)
    page_t = jnp.swapaxes(pages, 1, 2)

    smem = pl.BlockSpec(memory_space=pltpu.SMEM)
    vmem = pl.BlockSpec(memory_space=pltpu.VMEM)
    dq, slope, score = pl.pallas_call(
        grad_kernel,
        out_shape=(
            jax.ShapeDtypeStruct((n_query, n_tok, dim), jnp.bfloat16),
            jax.ShapeDtypeStruct((n_blocks, p_tok, width), jnp.bfloat16),
            jax.ShapeDtypeStruct((n_blocks, 1, width), jnp.float32),
        ),
        in_specs=[smem, smem] + [vmem] * 6,
        out_specs=(vmem, vmem, vmem),
        scratch_shapes=[
            pltpu.VMEM((width, dim), jnp.bfloat16),
            pltpu.VMEM((p_tok, width), jnp.float32),
            pltpu.VMEM((p_tok, width), jnp.float32),
            pltpu.VMEM((n_query, n_tok, dim), jnp.float32),
        ],
        compiler_params=pltpu.CompilerParams(vmem_limit_bytes=32 << 20),
        cost_estimate=pl.CostEstimate(flops=4 * 10**9, bytes_accessed=4 << 20, transcendentals=4 << 20),
        name="grad",
    )(order, blocks, gathered, pages, page_t, lanes(cnt), lanes(aim), diag)

    terms = lax.all_to_all(
        dq.reshape(n_dev, own, n_tok, dim), AXES, split_axis=0, concat_axis=0, tiled=True)

    page_grad = pl.pallas_call(
        page_kernel,
        out_shape=jax.ShapeDtypeStruct(pages.shape, pages.dtype),
        in_specs=[smem, smem, vmem, vmem],
        out_specs=vmem,
        scratch_shapes=[pltpu.VMEM((slots * n_tok, dim), jnp.bfloat16)],
        compiler_params=pltpu.CompilerParams(vmem_limit_bytes=32 << 20),
        cost_estimate=pl.CostEstimate(flops=2 * 10**9, bytes_accessed=4 << 20, transcendentals=0),
        name="page_part",
    )(order, blocks, gathered, slope)

    ranked = score.reshape(n_pages, slots, n_tok)[:, :, 0]
    found = place[:, :, None] == slot_ids[None, None, :]
    scores = jnp.sum(jnp.where(found & live[:, :, None], ranked[:, None, :], 0.0), axis=2)
    query_grad = jnp.sum(terms.astype(jnp.float32), axis=0)
    return scores, query_grad, page_grad


def solution(mesh):
    row = P(AXES)
    return jax.shard_map(
        body,
        mesh=mesh,
        in_specs=(P(AXES, None, None), P(AXES, None, None), P(AXES, None), row, P(AXES, None)),
        out_specs=(P(AXES, None), P(AXES, None, None), P(AXES, None, None)),
        check_vma=False,
    )
```

```python
import jax
import jax.numpy as jnp
from jax import lax
from jax.experimental import pallas as pl
from jax.experimental.pallas import tpu as pltpu
from jax.sharding import PartitionSpec as P

AXES = ("group", "member")
BLOCK = 8
LANES = 128
INV_TEMP = 20.0
LOG2E = 1.4426950408889634


def plan_kernel(count, users_ref, teacher_ref, table_ref, place_ref, cnt_ref, aim_ref):
    n_pages, slots = users_ref.shape
    width = cnt_ref.shape[2]
    per_page = cnt_ref.shape[0] // n_pages
    n_tok = width // BLOCK
    square = (LANES, LANES)
    pad = jnp.zeros((LANES - n_pages, slots), jnp.float32)
    side = jnp.zeros((LANES, LANES - slots), jnp.float32)
    wide = jnp.concatenate(
        [jnp.concatenate([users_ref[...].astype(jnp.float32), pad], axis=0), side], axis=1)
    tall = wide.T
    row = lax.broadcasted_iota(jnp.int32, (slots, LANES), 0)
    col = lax.broadcasted_iota(jnp.int32, (slots, LANES), 1)
    colf = col.astype(jnp.float32)
    teach = jnp.concatenate([teacher_ref[...], jnp.zeros((n_pages, LANES - slots), jnp.float32)], axis=1)
    spread_k = lax.broadcasted_iota(jnp.int32, (slots, slots * n_tok), 0)
    spread_l = lax.broadcasted_iota(jnp.int32, (slots, slots * n_tok), 1)
    spread = jnp.where((spread_l >= spread_k * n_tok) & (spread_l < (spread_k + 1) * n_tok), 1.0, 0.0)
    for p in range(n_pages):
        total = count[p]
        ucol = tall[0:slots, p:p + 1]
        urow = wide[p:p + 1, :]
        alive = (row < total) & (col < total)
        same = jnp.where((ucol == urow) & alive, 1.0, 0.0)
        before_c = jnp.sum(jnp.where(col < row, same, 0.0), axis=1, keepdims=True)
        before_r = jnp.sum(jnp.where(row < col, same, 0.0), axis=0, keepdims=True)
        first_c = (before_c == 0.0) & (row[:, 0:1] < total)
        first_r = (before_r == 0.0) & (col[0:1, :] < total)
        first_cf = jnp.where(first_c, 1.0, 0.0)
        first_rf = jnp.where(first_r, 1.0, 0.0)
        rank_c = jnp.sum(jnp.where(col < row, first_rf, 0.0), axis=1, keepdims=True)
        number = jnp.sum(first_rf, axis=1, keepdims=True)
        put = jnp.where(rank_c == colf, first_cf, 0.0)
        order = jnp.sum(put * ucol, axis=0, keepdims=True)
        hits = jnp.sum(same, axis=1, keepdims=True)
        aims = jnp.sum(same * teach[p:p + 1, :], axis=1, keepdims=True)
        cnt = jnp.sum(put * hits, axis=0, keepdims=True)
        aim = jnp.sum(put * aims, axis=0, keepdims=True)
        place = jnp.sum(same * (first_cf * rank_c), axis=0, keepdims=True)
        blocks = jnp.floor((number + (BLOCK - 1)) * (1.0 / BLOCK))
        entry = jnp.where(col[0:1, :] == slots, blocks, order)
        table_ref[p:p + 1, :] = entry.astype(jnp.int32)
        place_ref[p:p + 1, :] = jnp.where(col[0:1, :] < total, place, -1.0).astype(jnp.int32)
        both = jnp.concatenate([cnt, aim, jnp.zeros((6, LANES), jnp.float32)], axis=0)[:, 0:slots]
        lanes = jnp.dot(both, spread, precision=lax.Precision.HIGHEST,
                        preferred_element_type=jnp.float32)
        for j in range(per_page):
            cnt_ref[p * per_page + j] = lanes[0:1, j * width:(j + 1) * width]
            aim_ref[p * per_page + j] = lanes[1:2, j * width:(j + 1) * width]


def grad_kernel(table, q_ref, page_ref, page_t_ref, cnt_ref, aim_ref, place_ref,
                dq_hbm, slope_hbm, score_hbm,
                q2, qb, diag, sim, wts, moved, slope, acc, dq, shown, stat, sems, out_sem):
    n_pages, p_tok, dim = page_ref.shape
    n_tok = q_ref.shape[1]
    width = BLOCK * n_tok
    per_page = slope_hbm.shape[0] // n_pages
    slots = per_page * BLOCK
    chunk = 64
    parts = range(0, p_tok, chunk)
    scale_in = INV_TEMP * LOG2E
    share = 4
    quarters = p_tok // (share * chunk)
    always = table[0, slots] > 0

    def fold(x, op):
        x = x.reshape(x.shape[0] // 8, 8, width)
        out = x[0]
        for i in range(1, x.shape[0]):
            out = op(out, x[i])
        return out

    def flip(p, j):
        more = j + 1 < table[p, slots]
        last = p + 1 >= n_pages
        p2 = jnp.where(more, p, jnp.where(last, p, p + 1))
        j2 = jnp.where(more, j + 1, jnp.where(last, j, 0))
        return p2, j2

    def load_block(p, j):
        for k in range(BLOCK):
            qb[pl.ds(k * n_tok, n_tok), :] = q2[table[p, j * BLOCK + k]]

    def similar(p, n, top):
        rows = share * chunk
        tile = page_ref[p, n * rows:(n + 1) * rows, :]
        both = jnp.concatenate([tile, tile], axis=1)
        s = lax.dot_general(both, qb[...], (((1,), (1,)), ((), ())), preferred_element_type=jnp.float32)
        sim[n * rows:(n + 1) * rows, :] = s
        most = fold(s, jnp.maximum)
        return most if top is None else jnp.maximum(top, most)

    def add_part(p, j, part):
        part = part.T
        for k in range(BLOCK):
            acc[table[p, j * BLOCK + k]] += part[k * n_tok:(k + 1) * n_tok, :]

    def out_copy(b, slot):
        return pltpu.make_async_copy(slope.at[slot], slope_hbm.at[b], sems.at[slot])

    acc[...] = jnp.zeros_like(acc)
    shown[...] = jnp.zeros_like(shown)
    slope[1] = jnp.zeros((p_tok, width), slope.dtype)
    lane_i = lax.broadcasted_iota(jnp.int32, (width, width), 0) // n_tok
    lane_j = lax.broadcasted_iota(jnp.int32, (width, width), 1) // n_tok
    diag[...] = jnp.where(lane_i == lane_j, 1.0, 0.0).astype(jnp.bfloat16)
    wide = q_ref[...].astype(jnp.float32) * scale_in
    hi = wide.astype(jnp.bfloat16)
    q2[:, :, 0:dim] = hi
    q2[:, :, dim:2 * dim] = (wide - hi.astype(jnp.float32)).astype(jnp.bfloat16)
    load_block(0, 0)
    top = None
    for n in range(quarters):
        top = similar(0, n, top)
    stat[0] = top

    def step(t, carry):
        p0, j0, p, j = carry
        p2, j2 = flip(p, j)
        slot = lax.rem(t, 2)
        b = p * per_page + j

        @pl.when(always)
        def _():
            top = jnp.max(stat[0], axis=0, keepdims=True)
            total = jnp.zeros((8, width), jnp.float32)
            mass = jnp.zeros((8, width), jnp.float32)
            part = None
            for n, i in enumerate(parts):
                if n % share == 0:
                    k = n * chunk
                    term = jnp.dot(page_t_ref[p0, :, k:k + share * chunk], slope[1 - slot, k:k + share * chunk, :],
                                   preferred_element_type=jnp.float32)
                    part = term if part is None else part + term
                r = pl.ds(i, chunk)
                d = sim[r, :] - top
                e = jnp.exp2(d)
                v = e * d
                wts[r, :] = e
                moved[r, :] = v
                total += fold(e, jnp.add)
                mass += fold(v, jnp.add)
            add_part(p0, j0, part)
            stat[1] = total
            stat[2] = mass
            stat[3] = jnp.broadcast_to(top, (8, width))

        @pl.when(t >= 2)
        def _():
            out_copy(b, slot).wait()

        @pl.when(always)
        def _():
            inv = 1.0 / jnp.sum(stat[1], axis=0, keepdims=True)
            drift = jnp.sum(stat[2], axis=0, keepdims=True) * inv
            matched = (stat[3, 0:1, :] + drift) * (1.0 / scale_in)
            load_block(p2, j2)
            ahead = quarters // 2
            high = None
            for n in range(ahead):
                high = similar(p2, n, high)
            hi = matched.astype(jnp.bfloat16)
            rest = matched - hi.astype(jnp.float32)
            mid = rest.astype(jnp.bfloat16)
            low = (rest - mid.astype(jnp.float32)).astype(jnp.bfloat16)
            pieces = jnp.concatenate([hi, mid, low], axis=0)
            score = jnp.sum(
                jnp.dot(pieces, diag[...], preferred_element_type=jnp.float32), axis=0, keepdims=True)
            place = place_ref[pl.ds(p, 1), :]
            line = shown[pl.ds(p, 1), :]
            for k in range(BLOCK):
                part = score[:, (k * n_tok // LANES) * LANES:(k * n_tok // LANES + 1) * LANES]
                off = k * n_tok % LANES
                if off:
                    part = pltpu.roll(part, LANES - off, 1)
                line = jnp.where(place == j * BLOCK + k, part, line)
            shown[pl.ds(p, 1), :] = line
            scale = (cnt_ref[b] * score - aim_ref[b]) * inv
            beta = scale * (1.0 / LOG2E)
            alpha = scale - beta * drift
            for n, i in enumerate(parts):
                if n % share == 0 and n // share < quarters - ahead:
                    high = similar(p2, ahead + n // share, high)
                r = pl.ds(i, chunk)
                slope[slot, r, :] = (alpha * wts[r, :] + beta * moved[r, :]).astype(jnp.bfloat16)

            stat[0] = high

        out_copy(b, slot).start()
        return p, j, p2, j2

    count = table[0, slots]
    for p in range(1, n_pages):
        count += table[p, slots]
    zero = jnp.int32(0)
    p, j, _, _ = lax.fori_loop(0, count, step, (zero, zero, zero, zero))
    add_part(p, j, jnp.dot(page_t_ref[p], slope[lax.rem(count - 1, 2)], preferred_element_type=jnp.float32))
    dq[...] = acc[...].astype(dq.dtype)
    dq_copy = pltpu.make_async_copy(dq, dq_hbm, out_sem.at[0])
    score_copy = pltpu.make_async_copy(shown, score_hbm, out_sem.at[1])
    dq_copy.start()
    score_copy.start()
    out_copy(0, 0).wait()
    out_copy(0, 1).wait()
    dq_copy.wait()
    score_copy.wait()


def page_kernel(table, q_ref, slope_hbm, out_hbm, qb, buf, out, sems, out_sems):
    n_pages, p_tok, dim = out_hbm.shape
    n_tok = q_ref.shape[1]
    width = BLOCK * n_tok
    per_page = slope_hbm.shape[0] // n_pages
    slots = per_page * BLOCK

    def fetch(p, j):
        return pltpu.make_async_copy(
            slope_hbm.at[p * per_page + j], buf.at[p % 2, j], sems.at[p % 2, j])

    def store(p):
        return pltpu.make_async_copy(out.at[p % 2], out_hbm.at[p], out_sems.at[p % 2])

    def start(p):
        for j in range(per_page):
            @pl.when(j < table[p, slots])
            def _():
                fetch(p, j).start()

    start(0)
    for p in range(n_pages):
        if p + 1 < n_pages:
            start(p + 1)
        if p >= 2:
            store(p - 2).wait()
        for k in range(slots):
            qb[pl.ds(k * n_tok, n_tok), :] = q_ref[table[p, k]]
        for n in range(1, per_page + 1):
            @pl.when(table[p, slots] == n)
            def _():
                total = None
                for j in range(n):
                    fetch(p, j).wait()
                    term = jnp.dot(buf[p % 2, j], qb[pl.ds(j * width, width), :],
                                   preferred_element_type=jnp.float32)
                    total = term if total is None else total + term
                out[p % 2] = total.astype(out.dtype)
        store(p).start()
    for p in range(max(n_pages - 2, 0), n_pages):
        store(p).wait()


def body(queries, pages, users, page_count, teacher):
    n_dev = lax.axis_size("group") * lax.axis_size("member")
    own, n_tok, dim = queries.shape
    n_pages, p_tok, _ = pages.shape
    slots = users.shape[1]
    n_query = n_dev * own
    per_page = slots // BLOCK
    n_blocks = n_pages * per_page
    width = BLOCK * n_tok
    smem = pl.BlockSpec(memory_space=pltpu.SMEM)
    vmem = pl.BlockSpec(memory_space=pltpu.VMEM)
    hbm = pl.BlockSpec(memory_space=pl.ANY)

    copies = jnp.broadcast_to(queries[None], (n_dev, own, n_tok, dim))
    gathered = lax.all_to_all(copies, AXES, split_axis=0, concat_axis=0, tiled=True)
    gathered = gathered.reshape(n_query, n_tok, dim)
    page_t = jnp.swapaxes(pages, 1, 2)

    table, place, cnt, aim = pl.pallas_call(
        plan_kernel,
        out_shape=(
            jax.ShapeDtypeStruct((n_pages, LANES), jnp.int32),
            jax.ShapeDtypeStruct((n_pages, LANES), jnp.int32),
            jax.ShapeDtypeStruct((n_blocks, 1, width), jnp.float32),
            jax.ShapeDtypeStruct((n_blocks, 1, width), jnp.float32),
        ),
        in_specs=[smem, vmem, vmem],
        out_specs=(vmem,) * 4,
        compiler_params=pltpu.CompilerParams(vmem_limit_bytes=16 << 20),
        cost_estimate=pl.CostEstimate(flops=10**6, bytes_accessed=1 << 16, transcendentals=0),
        name="plan",
    )(page_count, users, teacher)

    dq, slope, scores = pl.pallas_call(
        grad_kernel,
        out_shape=(
            jax.ShapeDtypeStruct((n_query, n_tok, dim), jnp.bfloat16),
            jax.ShapeDtypeStruct((n_blocks, p_tok, width), jnp.bfloat16),
            jax.ShapeDtypeStruct((n_pages, LANES), jnp.float32),
        ),
        in_specs=[smem] + [vmem] * 6,
        out_specs=(hbm, hbm, hbm),
        scratch_shapes=[
            pltpu.VMEM((n_query, n_tok, 2 * dim), jnp.bfloat16),
            pltpu.VMEM((width, 2 * dim), jnp.bfloat16),
            pltpu.VMEM((width, width), jnp.bfloat16),
            pltpu.VMEM((p_tok, width), jnp.float32),
            pltpu.VMEM((p_tok, width), jnp.float32),
            pltpu.VMEM((p_tok, width), jnp.float32),
            pltpu.VMEM((2, p_tok, width), jnp.bfloat16),
            pltpu.VMEM((n_query, n_tok, dim), jnp.float32),
            pltpu.VMEM((n_query, n_tok, dim), jnp.bfloat16),
            pltpu.VMEM((n_pages, LANES), jnp.float32),
            pltpu.VMEM((4, 8, width), jnp.float32),
            pltpu.SemaphoreType.DMA((2,)),
            pltpu.SemaphoreType.DMA((2,)),
        ],
        compiler_params=pltpu.CompilerParams(vmem_limit_bytes=48 << 20),
        cost_estimate=pl.CostEstimate(flops=4 * 10**9, bytes_accessed=16 << 20, transcendentals=4 << 20),
        name="grad",
    )(table, gathered, pages, page_t, cnt, aim, place)

    terms = lax.all_to_all(
        dq.reshape(n_dev, own, n_tok, dim), AXES, split_axis=0, concat_axis=0, tiled=True)

    page_grad = pl.pallas_call(
        page_kernel,
        out_shape=jax.ShapeDtypeStruct(pages.shape, pages.dtype),
        in_specs=[smem, vmem, hbm],
        out_specs=hbm,
        scratch_shapes=[
            pltpu.VMEM((slots * n_tok, dim), jnp.bfloat16),
            pltpu.VMEM((2, per_page, p_tok, width), jnp.bfloat16),
            pltpu.VMEM((2, p_tok, dim), jnp.bfloat16),
            pltpu.SemaphoreType.DMA((2, per_page)),
            pltpu.SemaphoreType.DMA((2,)),
        ],
        compiler_params=pltpu.CompilerParams(vmem_limit_bytes=48 << 20),
        cost_estimate=pl.CostEstimate(flops=2 * 10**9, bytes_accessed=16 << 20, transcendentals=0),
        name="page_part",
    )(table, gathered, slope)

    query_grad = jnp.sum(terms.astype(jnp.float32), axis=0)
    return scores[:, :slots], query_grad, page_grad


def solution(mesh):
    return jax.shard_map(
        body,
        mesh=mesh,
        in_specs=(P(AXES, None, None), P(AXES, None, None), P(AXES, None), P(AXES), P(AXES, None)),
        out_specs=(P(AXES, None), P(AXES, None, None), P(AXES, None, None)),
        check_vma=False,
    )
```

```python
import jax
import jax.numpy as jnp
from jax import lax
from jax.experimental import pallas as pl
from jax.experimental.pallas import tpu as pltpu
from jax.sharding import PartitionSpec as P

AXES = ("group", "member")
BLOCK = 8
LANES = 128
INV_TEMP = 20.0
LOG2E = 1.4426950408889634


def plan_kernel(count, users_ref, teacher_ref, table_ref, place_ref, cnt_ref, aim_ref):
    n_pages, slots = users_ref.shape
    width = cnt_ref.shape[2]
    per_page = cnt_ref.shape[0] // n_pages
    n_tok = width // BLOCK
    square = (LANES, LANES)
    pad = jnp.zeros((LANES - n_pages, slots), jnp.float32)
    side = jnp.zeros((LANES, LANES - slots), jnp.float32)
    wide = jnp.concatenate(
        [jnp.concatenate([users_ref[...].astype(jnp.float32), pad], axis=0), side], axis=1)
    tall = wide.T
    row = lax.broadcasted_iota(jnp.int32, (slots, LANES), 0)
    col = lax.broadcasted_iota(jnp.int32, (slots, LANES), 1)
    colf = col.astype(jnp.float32)
    teach = jnp.concatenate([teacher_ref[...], jnp.zeros((n_pages, LANES - slots), jnp.float32)], axis=1)
    spread_k = lax.broadcasted_iota(jnp.int32, (slots, slots * n_tok), 0)
    spread_l = lax.broadcasted_iota(jnp.int32, (slots, slots * n_tok), 1)
    spread = jnp.where((spread_l >= spread_k * n_tok) & (spread_l < (spread_k + 1) * n_tok), 1.0, 0.0)
    for p in range(n_pages):
        total = count[p]
        ucol = tall[0:slots, p:p + 1]
        urow = wide[p:p + 1, :]
        alive = (row < total) & (col < total)
        same = jnp.where((ucol == urow) & alive, 1.0, 0.0)
        before_c = jnp.sum(jnp.where(col < row, same, 0.0), axis=1, keepdims=True)
        before_r = jnp.sum(jnp.where(row < col, same, 0.0), axis=0, keepdims=True)
        first_c = (before_c == 0.0) & (row[:, 0:1] < total)
        first_r = (before_r == 0.0) & (col[0:1, :] < total)
        first_cf = jnp.where(first_c, 1.0, 0.0)
        first_rf = jnp.where(first_r, 1.0, 0.0)
        rank_c = jnp.sum(jnp.where(col < row, first_rf, 0.0), axis=1, keepdims=True)
        number = jnp.sum(first_rf, axis=1, keepdims=True)
        put = jnp.where(rank_c == colf, first_cf, 0.0)
        order = jnp.sum(put * ucol, axis=0, keepdims=True)
        hits = jnp.sum(same, axis=1, keepdims=True)
        aims = jnp.sum(same * teach[p:p + 1, :], axis=1, keepdims=True)
        cnt = jnp.sum(put * hits, axis=0, keepdims=True)
        aim = jnp.sum(put * aims, axis=0, keepdims=True)
        place = jnp.sum(same * (first_cf * rank_c), axis=0, keepdims=True)
        blocks = jnp.floor((number + (BLOCK - 1)) * (1.0 / BLOCK))
        entry = jnp.where(col[0:1, :] == slots, blocks, order)
        table_ref[p:p + 1, :] = entry.astype(jnp.int32)
        place_ref[p:p + 1, :] = jnp.where(col[0:1, :] < total, place, -1.0).astype(jnp.int32)
        both = jnp.concatenate([cnt, aim, jnp.zeros((6, LANES), jnp.float32)], axis=0)[:, 0:slots]
        lanes = jnp.dot(both, spread, precision=lax.Precision.HIGHEST,
                        preferred_element_type=jnp.float32)
        for j in range(per_page):
            cnt_ref[p * per_page + j] = lanes[0:1, j * width:(j + 1) * width]
            aim_ref[p * per_page + j] = lanes[1:2, j * width:(j + 1) * width]


def grad_kernel(table, q_ref, page_ref, page_t_ref, cnt_ref, aim_ref, place_ref,
                dq_hbm, slope_hbm, score_hbm,
                q2, qb, diag, sim, wts, moved, slope, acc, dq, shown, stat, sems, out_sem):
    n_pages, p_tok, dim = page_ref.shape
    n_tok = q_ref.shape[1]
    width = BLOCK * n_tok
    per_page = slope_hbm.shape[0] // n_pages
    slots = per_page * BLOCK
    chunk = 64
    parts = range(0, p_tok, chunk)
    scale_in = INV_TEMP * LOG2E
    share = 4
    quarters = p_tok // (share * chunk)
    always = table[0, slots] > 0

    def fold(x, op):
        x = x.reshape(x.shape[0] // 8, 8, width)
        out = x[0]
        for i in range(1, x.shape[0]):
            out = op(out, x[i])
        return out

    def flip(p, j):
        more = j + 1 < table[p, slots]
        last = p + 1 >= n_pages
        p2 = jnp.where(more, p, jnp.where(last, p, p + 1))
        j2 = jnp.where(more, j + 1, jnp.where(last, j, 0))
        return p2, j2

    def load_block(p, j):
        for k in range(BLOCK):
            qb[pl.ds(k * n_tok, n_tok), :] = q2[table[p, j * BLOCK + k]]

    def similar(p, n, top):
        rows = share * chunk
        tile = page_ref[p, n * rows:(n + 1) * rows, :]
        both = jnp.concatenate([tile, tile], axis=1)
        s = lax.dot_general(both, qb[...], (((1,), (1,)), ((), ())), preferred_element_type=jnp.float32)
        sim[n * rows:(n + 1) * rows, :] = s
        most = fold(s, jnp.maximum)
        return most if top is None else jnp.maximum(top, most)

    def add_part(p, j, part):
        part = part.T
        for k in range(BLOCK):
            acc[table[p, j * BLOCK + k]] += part[k * n_tok:(k + 1) * n_tok, :]

    def out_copy(b, slot):
        return pltpu.make_async_copy(slope.at[slot], slope_hbm.at[b], sems.at[slot])

    acc[...] = jnp.zeros_like(acc)
    shown[...] = jnp.zeros_like(shown)
    lane_i = lax.broadcasted_iota(jnp.int32, (width, width), 0) // n_tok
    lane_j = lax.broadcasted_iota(jnp.int32, (width, width), 1) // n_tok
    diag[...] = jnp.where(lane_i == lane_j, 1.0, 0.0).astype(jnp.bfloat16)

    def split_step(i, c):
        for k in range(BLOCK):
            wide = q_ref[i * BLOCK + k].astype(jnp.float32) * scale_in
            hi = wide.astype(jnp.bfloat16)
            q2[i * BLOCK + k, :, 0:dim] = hi
            q2[i * BLOCK + k, :, dim:2 * dim] = (wide - hi.astype(jnp.float32)).astype(jnp.bfloat16)
        return c
    lax.fori_loop(0, q_ref.shape[0] // BLOCK, split_step, 0)
    load_block(0, 0)
    top = None
    for n in range(quarters):
        top = similar(0, n, top)
    stat[0] = top

    def step(t, carry):
        p0, j0, p, j = carry
        p2, j2 = flip(p, j)
        slot = lax.rem(t, 2)
        b = p * per_page + j

        @pl.when(always)
        def _():
            top = jnp.max(stat[0], axis=0, keepdims=True)
            total = jnp.zeros((8, width), jnp.float32)
            mass = jnp.zeros((8, width), jnp.float32)
            part = None
            for n, i in enumerate(parts):
                if n % share == 0:
                    k = n * chunk
                    term = jnp.dot(page_t_ref[p0, :, k:k + share * chunk], slope[1 - slot, k:k + share * chunk, :],
                                   preferred_element_type=jnp.float32)
                    part = term if part is None else part + term
                r = pl.ds(i, chunk)
                d = sim[r, :] - top
                e = jnp.exp2(d)
                v = e * d
                wts[r, :] = e
                moved[r, :] = v
                total += fold(e, jnp.add)
                mass += fold(v, jnp.add)
            add_part(p0, j0, jnp.where(t >= 1, part, 0.0))
            stat[1] = total
            stat[2] = mass
            stat[3] = jnp.broadcast_to(top, (8, width))

        @pl.when(t >= 2)
        def _():
            out_copy(b, slot).wait()

        @pl.when(always)
        def _():
            inv = 1.0 / jnp.sum(stat[1], axis=0, keepdims=True)
            drift = jnp.sum(stat[2], axis=0, keepdims=True) * inv
            matched = (stat[3, 0:1, :] + drift) * (1.0 / scale_in)
            load_block(p2, j2)
            ahead = 1
            high = None
            for n in range(ahead):
                high = similar(p2, n, high)
            hi = matched.astype(jnp.bfloat16)
            rest = matched - hi.astype(jnp.float32)
            mid = rest.astype(jnp.bfloat16)
            low = (rest - mid.astype(jnp.float32)).astype(jnp.bfloat16)
            pieces = jnp.concatenate([hi, mid, low], axis=0)
            score = jnp.sum(
                jnp.dot(pieces, diag[...], preferred_element_type=jnp.float32), axis=0, keepdims=True)
            place = place_ref[pl.ds(p, 1), :]
            line = shown[pl.ds(p, 1), :]
            for k in range(BLOCK):
                part = score[:, (k * n_tok // LANES) * LANES:(k * n_tok // LANES + 1) * LANES]
                off = k * n_tok % LANES
                if off:
                    part = pltpu.roll(part, LANES - off, 1)
                line = jnp.where(place == j * BLOCK + k, part, line)
            shown[pl.ds(p, 1), :] = line
            scale = (cnt_ref[b] * score - aim_ref[b]) * inv
            beta = scale * (1.0 / LOG2E)
            alpha = scale - beta * drift
            for n, i in enumerate(parts):
                if n % share == 0 and n // share < quarters - ahead:
                    high = similar(p2, ahead + n // share, high)
                r = pl.ds(i, chunk)
                y = alpha * wts[r, :] + beta * moved[r, :]
                slope[slot, r, :] = y.astype(jnp.bfloat16)
            stat[4] = high + y[0:8, :]
            stat[0] = high

        out_copy(b, slot).start()
        return p, j, p2, j2

    count = table[0, slots]
    for p in range(1, n_pages):
        count += table[p, slots]
    zero = jnp.int32(0)
    p, j, _, _ = lax.fori_loop(0, count, step, (zero, zero, zero, zero))
    add_part(p, j, jnp.dot(page_t_ref[p], slope[lax.rem(count - 1, 2)], preferred_element_type=jnp.float32))
    dq[...] = acc[...].astype(dq.dtype)
    dq_copy = pltpu.make_async_copy(dq, dq_hbm, out_sem.at[0])
    score_copy = pltpu.make_async_copy(shown, score_hbm, out_sem.at[1])
    dq_copy.start()
    score_copy.start()
    out_copy(0, 0).wait()
    out_copy(0, 1).wait()
    dq_copy.wait()
    score_copy.wait()


def page_kernel(table, q_ref, slope_hbm, out_hbm, qb, buf, out, sems, out_sems):
    n_pages, p_tok, dim = out_hbm.shape
    n_tok = q_ref.shape[1]
    width = BLOCK * n_tok
    per_page = slope_hbm.shape[0] // n_pages
    slots = per_page * BLOCK

    def fetch(b):
        return pltpu.make_async_copy(slope_hbm.at[b], buf.at[b], sems.at[b])

    def store(p, slot):
        return pltpu.make_async_copy(out.at[slot], out_hbm.at[p], out_sems.at[slot])

    for p in range(n_pages):
        for j in range(per_page):
            @pl.when(j < table[p, slots])
            def _():
                fetch(p * per_page + j).start()

    def page_step(p, c):
        slot = lax.rem(p, 2)
        number = table[p, slots]

        @pl.when(p >= 2)
        def _():
            store(p, slot).wait()
        for n in range(1, per_page + 1):
            @pl.when(number == n)
            def _():
                total = None
                for k in range(n * BLOCK):
                    qb[pl.ds(k * n_tok, n_tok), :] = q_ref[table[p, k]]
                for j in range(n):
                    fetch(p * per_page + j).wait()
                for j in range(n):
                    term = jnp.dot(buf[p * per_page + j], qb[pl.ds(j * width, width), :],
                                   preferred_element_type=jnp.float32)
                    total = term if total is None else total + term
                out[slot] = total.astype(out.dtype)
        store(p, slot).start()
        return c
    lax.fori_loop(0, n_pages, page_step, 0)
    for p in range(max(n_pages - 2, 0), n_pages):
        store(p, p % 2).wait()


def body(queries, pages, users, page_count, teacher):
    n_dev = lax.axis_size("group") * lax.axis_size("member")
    own, n_tok, dim = queries.shape
    n_pages, p_tok, _ = pages.shape
    slots = users.shape[1]
    n_query = n_dev * own
    per_page = slots // BLOCK
    n_blocks = n_pages * per_page
    width = BLOCK * n_tok
    smem = pl.BlockSpec(memory_space=pltpu.SMEM)
    vmem = pl.BlockSpec(memory_space=pltpu.VMEM)
    hbm = pl.BlockSpec(memory_space=pl.ANY)

    copies = jnp.broadcast_to(queries[None], (n_dev, own, n_tok, dim))
    gathered = lax.all_to_all(copies, AXES, split_axis=0, concat_axis=0, tiled=True)
    gathered = gathered.reshape(n_query, n_tok, dim)
    page_t = jnp.swapaxes(pages, 1, 2)

    table, place, cnt, aim = pl.pallas_call(
        plan_kernel,
        out_shape=(
            jax.ShapeDtypeStruct((n_pages, LANES), jnp.int32),
            jax.ShapeDtypeStruct((n_pages, LANES), jnp.int32),
            jax.ShapeDtypeStruct((n_blocks, 1, width), jnp.float32),
            jax.ShapeDtypeStruct((n_blocks, 1, width), jnp.float32),
        ),
        in_specs=[smem, vmem, vmem],
        out_specs=(vmem,) * 4,
        compiler_params=pltpu.CompilerParams(vmem_limit_bytes=16 << 20),
        cost_estimate=pl.CostEstimate(flops=10**6, bytes_accessed=1 << 16, transcendentals=0),
        name="plan",
    )(page_count, users, teacher)

    dq, slope, scores = pl.pallas_call(
        grad_kernel,
        out_shape=(
            jax.ShapeDtypeStruct((n_query, n_tok, dim), jnp.bfloat16),
            jax.ShapeDtypeStruct((n_blocks, p_tok, width), jnp.bfloat16),
            jax.ShapeDtypeStruct((n_pages, LANES), jnp.float32),
        ),
        in_specs=[smem] + [vmem] * 6,
        out_specs=(hbm, hbm, hbm),
        scratch_shapes=[
            pltpu.VMEM((n_query, n_tok, 2 * dim), jnp.bfloat16),
            pltpu.VMEM((width, 2 * dim), jnp.bfloat16),
            pltpu.VMEM((width, width), jnp.bfloat16),
            pltpu.VMEM((p_tok, width), jnp.float32),
            pltpu.VMEM((p_tok, width), jnp.float32),
            pltpu.VMEM((p_tok, width), jnp.float32),
            pltpu.VMEM((2, p_tok, width), jnp.bfloat16),
            pltpu.VMEM((n_query, n_tok, dim), jnp.float32),
            pltpu.VMEM((n_query, n_tok, dim), jnp.bfloat16),
            pltpu.VMEM((n_pages, LANES), jnp.float32),
            pltpu.VMEM((6, 8, width), jnp.float32),
            pltpu.SemaphoreType.DMA((2,)),
            pltpu.SemaphoreType.DMA((2,)),
        ],
        compiler_params=pltpu.CompilerParams(vmem_limit_bytes=48 << 20),
        cost_estimate=pl.CostEstimate(flops=4 * 10**9, bytes_accessed=16 << 20, transcendentals=4 << 20),
        name="grad",
    )(table, gathered, pages, page_t, cnt, aim, place)

    terms = lax.all_to_all(
        dq.reshape(n_dev, own, n_tok, dim), AXES, split_axis=0, concat_axis=0, tiled=True)

    page_grad = pl.pallas_call(
        page_kernel,
        out_shape=jax.ShapeDtypeStruct(pages.shape, pages.dtype),
        in_specs=[smem, vmem, hbm],
        out_specs=hbm,
        scratch_shapes=[
            pltpu.VMEM((slots * n_tok, dim), jnp.bfloat16),
            pltpu.VMEM((n_blocks, p_tok, width), jnp.bfloat16),
            pltpu.VMEM((2, p_tok, dim), jnp.bfloat16),
            pltpu.SemaphoreType.DMA((n_blocks,)),
            pltpu.SemaphoreType.DMA((2,)),
        ],
        compiler_params=pltpu.CompilerParams(vmem_limit_bytes=48 << 20),
        cost_estimate=pl.CostEstimate(flops=2 * 10**9, bytes_accessed=16 << 20, transcendentals=0),
        name="page_part",
    )(table, gathered, slope)

    query_grad = jnp.sum(terms.astype(jnp.float32), axis=0)
    return scores[:, :slots], query_grad, page_grad


def solution(mesh):
    return jax.shard_map(
        body,
        mesh=mesh,
        in_specs=(P(AXES, None, None), P(AXES, None, None), P(AXES, None), P(AXES), P(AXES, None)),
        out_specs=(P(AXES, None), P(AXES, None, None), P(AXES, None, None)),
        check_vma=False,
    )
```

```python
import jax
import jax.numpy as jnp
from jax import lax
from jax.experimental import pallas as pl
from jax.experimental.pallas import tpu as pltpu
from jax.sharding import PartitionSpec as P

AXES = ("group", "member")
BLOCK = 8
LANES = 128
INV_TEMP = 20.0
LOG2E = 1.4426950408889634


def plan_kernel(count, users_ref, teacher_ref, table_ref, place_ref, cnt_ref, aim_ref):
    n_pages, slots = users_ref.shape
    width = cnt_ref.shape[2]
    per_page = cnt_ref.shape[0] // n_pages
    n_tok = width // BLOCK
    square = (LANES, LANES)
    pad = jnp.zeros((LANES - n_pages, slots), jnp.float32)
    side = jnp.zeros((LANES, LANES - slots), jnp.float32)
    wide = jnp.concatenate(
        [jnp.concatenate([users_ref[...].astype(jnp.float32), pad], axis=0), side], axis=1)
    tall = wide.T
    row = lax.broadcasted_iota(jnp.int32, (slots, LANES), 0)
    col = lax.broadcasted_iota(jnp.int32, (slots, LANES), 1)
    colf = col.astype(jnp.float32)
    teach = jnp.concatenate([teacher_ref[...], jnp.zeros((n_pages, LANES - slots), jnp.float32)], axis=1)
    spread_k = lax.broadcasted_iota(jnp.int32, (slots, slots * n_tok), 0)
    spread_l = lax.broadcasted_iota(jnp.int32, (slots, slots * n_tok), 1)
    spread = jnp.where((spread_l >= spread_k * n_tok) & (spread_l < (spread_k + 1) * n_tok), 1.0, 0.0)
    for p in range(n_pages):
        total = count[p]
        ucol = tall[0:slots, p:p + 1]
        urow = wide[p:p + 1, :]
        alive = (row < total) & (col < total)
        same = jnp.where((ucol == urow) & alive, 1.0, 0.0)
        before_c = jnp.sum(jnp.where(col < row, same, 0.0), axis=1, keepdims=True)
        before_r = jnp.sum(jnp.where(row < col, same, 0.0), axis=0, keepdims=True)
        first_c = (before_c == 0.0) & (row[:, 0:1] < total)
        first_r = (before_r == 0.0) & (col[0:1, :] < total)
        first_cf = jnp.where(first_c, 1.0, 0.0)
        first_rf = jnp.where(first_r, 1.0, 0.0)
        rank_c = jnp.sum(jnp.where(col < row, first_rf, 0.0), axis=1, keepdims=True)
        number = jnp.sum(first_rf, axis=1, keepdims=True)
        put = jnp.where(rank_c == colf, first_cf, 0.0)
        order = jnp.sum(put * ucol, axis=0, keepdims=True)
        hits = jnp.sum(same, axis=1, keepdims=True)
        aims = jnp.sum(same * teach[p:p + 1, :], axis=1, keepdims=True)
        cnt = jnp.sum(put * hits, axis=0, keepdims=True)
        aim = jnp.sum(put * aims, axis=0, keepdims=True)
        place = jnp.sum(same * (first_cf * rank_c), axis=0, keepdims=True)
        blocks = jnp.floor((number + (BLOCK - 1)) * (1.0 / BLOCK))
        entry = jnp.where(col[0:1, :] == slots, blocks, order)
        table_ref[p:p + 1, :] = entry.astype(jnp.int32)
        place_ref[p:p + 1, :] = jnp.where(col[0:1, :] < total, place, -1.0).astype(jnp.int32)
        both = jnp.concatenate([cnt, aim, jnp.zeros((6, LANES), jnp.float32)], axis=0)[:, 0:slots]
        lanes = jnp.dot(both, spread, precision=lax.Precision.HIGHEST,
                        preferred_element_type=jnp.float32)
        for j in range(per_page):
            cnt_ref[p * per_page + j] = lanes[0:1, j * width:(j + 1) * width]
            aim_ref[p * per_page + j] = lanes[1:2, j * width:(j + 1) * width]


def grad_kernel(table_ref, q_ref, page_ref, page_t_ref, cnt_ref, aim_ref, place_ref, spent_hbm,
                dq_hbm, slope_hbm, score_hbm,
                q2, qb, diag, held, sim, wts, moved, slope, acc, dq, shown, stat, table, sems, out_sem):
    n_pages, p_tok, dim = page_ref.shape
    n_tok = q_ref.shape[1]
    width = BLOCK * n_tok
    per_page = slope_hbm.shape[0] // n_pages
    slots = per_page * BLOCK
    chunk = 64
    parts = range(0, p_tok, chunk)
    scale_in = INV_TEMP * LOG2E
    share = 4
    quarters = p_tok // (share * chunk)

    def fold(x, op):
        x = x.reshape(x.shape[0] // 8, 8, width)
        out = x[0]
        for i in range(1, x.shape[0]):
            out = op(out, x[i])
        return out

    def flip(p, j):
        more = j + 1 < table[p, slots]
        last = p + 1 >= n_pages
        p2 = jnp.where(more, p, jnp.where(last, p, p + 1))
        j2 = jnp.where(more, j + 1, jnp.where(last, j, 0))
        return p2, j2

    def load_block(p, j):
        tie = None
        for k in range(BLOCK):
            rows = q2[table[p, j * BLOCK + k]]
            qb[pl.ds(k * n_tok, n_tok), :] = rows
            tie = rows[0:8, :] if tie is None else tie + rows[0:8, :]
        return tie.astype(jnp.float32)

    def similar(p, n, top):
        rows = share * chunk
        tile = page_ref[p, n * rows:(n + 1) * rows, :]
        both = jnp.concatenate([tile, tile], axis=1)
        s = lax.dot_general(both, qb[...], (((1,), (1,)), ((), ())), preferred_element_type=jnp.float32)
        sim[n * rows:(n + 1) * rows, :] = s
        most = fold(s, jnp.maximum)
        return most if top is None else jnp.maximum(top, most)

    def add_part(p, j, part):
        part = part.T
        for k in range(BLOCK):
            acc[table[p, j * BLOCK + k]] += part[k * n_tok:(k + 1) * n_tok, :]
        return part

    def out_copy(b, slot):
        return pltpu.make_async_copy(slope.at[slot], slope_hbm.at[b], sems.at[slot])

    fetch = pltpu.make_async_copy(table_ref, table, out_sem.at[2])
    fetch.start()
    acc[...] = jnp.zeros_like(acc)
    shown[...] = jnp.zeros_like(shown)
    lane_i = lax.broadcasted_iota(jnp.int32, (width, width), 0) // n_tok
    lane_j = lax.broadcasted_iota(jnp.int32, (width, width), 1) // n_tok
    diag[...] = jnp.where(lane_i == lane_j, 1.0, 0.0).astype(jnp.bfloat16)

    def split_step(i, c):
        for k in range(BLOCK):
            wide = q_ref[i * BLOCK + k].astype(jnp.float32) * scale_in
            hi = wide.astype(jnp.bfloat16)
            q2[i * BLOCK + k, :, 0:dim] = hi
            q2[i * BLOCK + k, :, dim:2 * dim] = (wide - hi.astype(jnp.float32)).astype(jnp.bfloat16)
        return c
    lax.fori_loop(0, q_ref.shape[0] // BLOCK, split_step, 0)
    fetch.wait()
    always = table[0, slots] > 0
    load_block(0, 0)
    top = None
    for n in range(quarters):
        top = similar(0, n, top)
    stat[0] = top

    def step(t, carry):
        p0, j0, p, j = carry
        p2, j2 = flip(p, j)
        slot = lax.rem(t, 2)
        b = p * per_page + j

        @pl.when(always)
        def _():
            tie = load_block(p2, j2)
            top = jnp.max(stat[0], axis=0, keepdims=True)
            total = jnp.zeros((8, width), jnp.float32)
            mass = jnp.zeros((8, width), jnp.float32)
            part = None
            for n, i in enumerate(parts):
                if n % share == 0:
                    k = n * chunk
                    term = jnp.dot(page_t_ref[p0, :, k:k + share * chunk], slope[1 - slot, k:k + share * chunk, :],
                                   preferred_element_type=jnp.float32)
                    part = term if part is None else part + term
                r = pl.ds(i, chunk)
                d = sim[r, :] - top
                e = jnp.exp2(d)
                v = e * d
                wts[r, :] = e
                moved[r, :] = v
                total += fold(e, jnp.add)
                mass += fold(v, jnp.add)
            held[...] = part
            stat[1] = total
            stat[5] = total + tie
            stat[2] = mass
            stat[3] = jnp.broadcast_to(top, (8, width))

        @pl.when(t >= 2)
        def _():
            out_copy(b, slot).wait()

        @pl.when(always)
        def _():
            inv = 1.0 / jnp.sum(stat[1], axis=0, keepdims=True)
            drift = jnp.sum(stat[2], axis=0, keepdims=True) * inv
            matched = (stat[3, 0:1, :] + drift) * (1.0 / scale_in)
            ahead = 1
            high = None
            for n in range(ahead):
                high = similar(p2, n, high)
            hi = matched.astype(jnp.bfloat16)
            rest = matched - hi.astype(jnp.float32)
            mid = rest.astype(jnp.bfloat16)
            low = (rest - mid.astype(jnp.float32)).astype(jnp.bfloat16)
            pieces = jnp.concatenate([hi, mid, low], axis=0)
            score = jnp.sum(
                jnp.dot(pieces, diag[...], preferred_element_type=jnp.float32), axis=0, keepdims=True)
            place = place_ref[pl.ds(p, 1), :]
            line = shown[pl.ds(p, 1), :]
            for k in range(BLOCK):
                part = score[:, (k * n_tok // LANES) * LANES:(k * n_tok // LANES + 1) * LANES]
                off = k * n_tok % LANES
                if off:
                    part = pltpu.roll(part, LANES - off, 1)
                line = jnp.where(place == j * BLOCK + k, part, line)
            shown[pl.ds(p, 1), :] = line
            scale = (cnt_ref[b] * score - aim_ref[b]) * inv
            beta = scale * (1.0 / LOG2E)
            alpha = scale - beta * drift
            for n, i in enumerate(parts):
                if n % share == 0 and n // share < quarters - ahead:
                    high = similar(p2, ahead + n // share, high)
                r = pl.ds(i, chunk)
                y = alpha * wts[r, :] + beta * moved[r, :]
                slope[slot, r, :] = y.astype(jnp.bfloat16)
            rows = add_part(p0, j0, jnp.where(t >= 1, held[...], 0.0))
            stat[4] = high + y[0:8, :]
            stat[4, :, 0:LANES] = y[0:8, 0:LANES] + rows[0:8, :]
            stat[0] = high

        out_copy(b, slot).start()
        return p, j, p2, j2

    count = table[0, slots]
    for p in range(1, n_pages):
        count += table[p, slots]
    zero = jnp.int32(0)
    p, j, _, _ = lax.fori_loop(0, count, step, (zero, zero, zero, zero))
    add_part(p, j, jnp.dot(page_t_ref[p], slope[lax.rem(count - 1, 2)], preferred_element_type=jnp.float32))
    dq[...] = acc[...].astype(dq.dtype)
    dq_copy = pltpu.make_async_copy(dq, dq_hbm, out_sem.at[0])
    score_copy = pltpu.make_async_copy(shown, score_hbm, out_sem.at[1])
    dq_copy.start()
    score_copy.start()
    out_copy(0, 0).wait()
    out_copy(0, 1).wait()
    dq_copy.wait()
    score_copy.wait()


def page_kernel(table, q_ref, slope_hbm, out_hbm, qb, buf, out, sems, out_sems):
    n_pages, p_tok, dim = out_hbm.shape
    n_tok = q_ref.shape[1]
    width = BLOCK * n_tok
    per_page = slope_hbm.shape[0] // n_pages
    slots = per_page * BLOCK

    def fetch(b):
        return pltpu.make_async_copy(slope_hbm.at[b], buf.at[b], sems.at[b])

    def store(p, slot):
        return pltpu.make_async_copy(out.at[slot], out_hbm.at[p], out_sems.at[slot])

    for p in range(n_pages):
        for j in range(per_page):
            @pl.when(j < table[p, slots])
            def _():
                fetch(p * per_page + j).start()

    def page_step(p, c):
        slot = lax.rem(p, 2)
        number = table[p, slots]

        @pl.when(p >= 2)
        def _():
            store(p, slot).wait()
        for n in range(1, per_page + 1):
            @pl.when(number == n)
            def _():
                total = None
                for k in range(n * BLOCK):
                    qb[pl.ds(k * n_tok, n_tok), :] = q_ref[table[p, k]]
                for j in range(n):
                    fetch(p * per_page + j).wait()
                for j in range(n):
                    term = jnp.dot(buf[p * per_page + j], qb[pl.ds(j * width, width), :],
                                   preferred_element_type=jnp.float32)
                    total = term if total is None else total + term
                out[slot] = total.astype(out.dtype)
        store(p, slot).start()
        return c
    lax.fori_loop(0, n_pages, page_step, 0)
    for p in range(max(n_pages - 2, 0), n_pages):
        store(p, p % 2).wait()


def body(queries, pages, users, page_count, teacher):
    n_dev = lax.axis_size("group") * lax.axis_size("member")
    own, n_tok, dim = queries.shape
    n_pages, p_tok, _ = pages.shape
    slots = users.shape[1]
    n_query = n_dev * own
    per_page = slots // BLOCK
    n_blocks = n_pages * per_page
    width = BLOCK * n_tok
    smem = pl.BlockSpec(memory_space=pltpu.SMEM)
    vmem = pl.BlockSpec(memory_space=pltpu.VMEM)
    hbm = pl.BlockSpec(memory_space=pltpu.HBM)

    copies = jnp.broadcast_to(queries[None], (n_dev, own, n_tok, dim))
    copies = lax.optimization_barrier(copies)
    gathered = lax.all_to_all(copies, AXES, split_axis=0, concat_axis=0, tiled=True)
    gathered = gathered.reshape(n_query, n_tok, dim)
    page_t = jnp.swapaxes(pages, 1, 2)

    table, place, cnt, aim = pl.pallas_call(
        plan_kernel,
        out_shape=(
            jax.ShapeDtypeStruct((n_pages, LANES), jnp.int32),
            jax.ShapeDtypeStruct((n_pages, LANES), jnp.int32),
            jax.ShapeDtypeStruct((n_blocks, 1, width), jnp.float32),
            jax.ShapeDtypeStruct((n_blocks, 1, width), jnp.float32),
        ),
        in_specs=[smem, vmem, vmem],
        out_specs=(vmem,) * 4,
        compiler_params=pltpu.CompilerParams(vmem_limit_bytes=16 << 20),
        cost_estimate=pl.CostEstimate(flops=10**6, bytes_accessed=1 << 16, transcendentals=0),
        name="plan",
    )(page_count, users, teacher)

    dq, slope, scores = pl.pallas_call(
        grad_kernel,
        out_shape=(
            jax.ShapeDtypeStruct((n_query, n_tok, dim), jnp.bfloat16),
            jax.ShapeDtypeStruct((n_blocks, p_tok, width), jnp.bfloat16),
            jax.ShapeDtypeStruct((n_pages, LANES), jnp.float32),
        ),
        in_specs=[vmem] * 7 + [hbm],
        out_specs=(hbm, hbm, hbm),
        input_output_aliases={7: 0},
        scratch_shapes=[
            pltpu.VMEM((n_query, n_tok, 2 * dim), jnp.bfloat16),
            pltpu.VMEM((width, 2 * dim), jnp.bfloat16),
            pltpu.VMEM((width, width), jnp.bfloat16),
            pltpu.VMEM((dim, width), jnp.float32),
            pltpu.VMEM((p_tok, width), jnp.float32),
            pltpu.VMEM((p_tok, width), jnp.float32),
            pltpu.VMEM((p_tok, width), jnp.float32),
            pltpu.VMEM((2, p_tok, width), jnp.bfloat16),
            pltpu.VMEM((n_query, n_tok, dim), jnp.float32),
            pltpu.VMEM((n_query, n_tok, dim), jnp.bfloat16),
            pltpu.VMEM((n_pages, LANES), jnp.float32),
            pltpu.VMEM((6, 8, width), jnp.float32),
            pltpu.SMEM((n_pages, LANES), jnp.int32),
            pltpu.SemaphoreType.DMA((2,)),
            pltpu.SemaphoreType.DMA((3,)),
        ],
        compiler_params=pltpu.CompilerParams(vmem_limit_bytes=48 << 20),
        cost_estimate=pl.CostEstimate(flops=4 * 10**9, bytes_accessed=16 << 20, transcendentals=4 << 20),
        name="grad",
    )(table, gathered, pages, page_t, cnt, aim, place, copies.reshape(n_query, n_tok, dim))

    terms = lax.all_to_all(
        dq.reshape(n_dev, own, n_tok, dim), AXES, split_axis=0, concat_axis=0, tiled=True)

    page_grad = pl.pallas_call(
        page_kernel,
        out_shape=jax.ShapeDtypeStruct(pages.shape, pages.dtype),
        in_specs=[smem, vmem, hbm],
        out_specs=hbm,
        scratch_shapes=[
            pltpu.VMEM((slots * n_tok, dim), jnp.bfloat16),
            pltpu.VMEM((n_blocks, p_tok, width), jnp.bfloat16),
            pltpu.VMEM((2, p_tok, dim), jnp.bfloat16),
            pltpu.SemaphoreType.DMA((n_blocks,)),
            pltpu.SemaphoreType.DMA((2,)),
        ],
        compiler_params=pltpu.CompilerParams(vmem_limit_bytes=48 << 20),
        cost_estimate=pl.CostEstimate(flops=2 * 10**9, bytes_accessed=16 << 20, transcendentals=0),
        name="page_part",
    )(table, gathered, slope)

    query_grad = jnp.sum(terms.astype(jnp.float32), axis=0)
    return scores[:, :slots], query_grad, page_grad


def solution(mesh):
    return jax.shard_map(
        body,
        mesh=mesh,
        in_specs=(P(AXES, None, None), P(AXES, None, None), P(AXES, None), P(AXES), P(AXES, None)),
        out_specs=(P(AXES, None), P(AXES, None, None), P(AXES, None, None)),
        check_vma=False,
    )
```

```python
import jax
import jax.numpy as jnp
from jax import lax
from jax.experimental import pallas as pl
from jax.experimental.pallas import tpu as pltpu
from jax.sharding import PartitionSpec as P

AXES = ("group", "member")
BLOCK = 8
LANES = 128
INV_TEMP = 20.0
LOG2E = 1.4426950408889634


def plan_kernel(count, users_ref, teacher_ref, table_ref, place_ref, cnt_ref, aim_ref):
    n_pages, slots = users_ref.shape
    width = cnt_ref.shape[2]
    per_page = cnt_ref.shape[0] // n_pages
    n_tok = width // BLOCK
    square = (LANES, LANES)
    pad = jnp.zeros((LANES - n_pages, slots), jnp.float32)
    side = jnp.zeros((LANES, LANES - slots), jnp.float32)
    wide = jnp.concatenate(
        [jnp.concatenate([users_ref[...].astype(jnp.float32), pad], axis=0), side], axis=1)
    tall = wide.T
    row = lax.broadcasted_iota(jnp.int32, (slots, LANES), 0)
    col = lax.broadcasted_iota(jnp.int32, (slots, LANES), 1)
    colf = col.astype(jnp.float32)
    teach = jnp.concatenate([teacher_ref[...], jnp.zeros((n_pages, LANES - slots), jnp.float32)], axis=1)
    spread_k = lax.broadcasted_iota(jnp.int32, (slots, slots * n_tok), 0)
    spread_l = lax.broadcasted_iota(jnp.int32, (slots, slots * n_tok), 1)
    spread = jnp.where((spread_l >= spread_k * n_tok) & (spread_l < (spread_k + 1) * n_tok), 1.0, 0.0)
    for p in range(n_pages):
        total = count[p]
        ucol = tall[0:slots, p:p + 1]
        urow = wide[p:p + 1, :]
        alive = (row < total) & (col < total)
        same = jnp.where((ucol == urow) & alive, 1.0, 0.0)
        before_c = jnp.sum(jnp.where(col < row, same, 0.0), axis=1, keepdims=True)
        before_r = jnp.sum(jnp.where(row < col, same, 0.0), axis=0, keepdims=True)
        first_c = (before_c == 0.0) & (row[:, 0:1] < total)
        first_r = (before_r == 0.0) & (col[0:1, :] < total)
        first_cf = jnp.where(first_c, 1.0, 0.0)
        first_rf = jnp.where(first_r, 1.0, 0.0)
        rank_c = jnp.sum(jnp.where(col < row, first_rf, 0.0), axis=1, keepdims=True)
        number = jnp.sum(first_rf, axis=1, keepdims=True)
        put = jnp.where(rank_c == colf, first_cf, 0.0)
        order = jnp.sum(put * ucol, axis=0, keepdims=True)
        hits = jnp.sum(same, axis=1, keepdims=True)
        aims = jnp.sum(same * teach[p:p + 1, :], axis=1, keepdims=True)
        cnt = jnp.sum(put * hits, axis=0, keepdims=True)
        aim = jnp.sum(put * aims, axis=0, keepdims=True)
        place = jnp.sum(same * (first_cf * rank_c), axis=0, keepdims=True)
        blocks = jnp.floor((number + (BLOCK - 1)) * (1.0 / BLOCK))
        entry = jnp.where(col[0:1, :] == slots, blocks, order)
        table_ref[p:p + 1, :] = entry.astype(jnp.int32)
        place_ref[p:p + 1, :] = jnp.where(col[0:1, :] < total, place, -1.0).astype(jnp.int32)
        both = jnp.concatenate([cnt, aim, jnp.zeros((6, LANES), jnp.float32)], axis=0)[:, 0:slots]
        lanes = jnp.dot(both, spread, precision=lax.Precision.HIGHEST,
                        preferred_element_type=jnp.float32)
        for j in range(per_page):
            cnt_ref[p * per_page + j] = lanes[0:1, j * width:(j + 1) * width]
            aim_ref[p * per_page + j] = lanes[1:2, j * width:(j + 1) * width]


def grad_kernel(table_ref, q_ref, page_ref, page_t_ref, cnt_ref, aim_ref, place_ref, spent_hbm,
                dq_hbm, slope_hbm, score_hbm,
                qb, diag, held, sim, wts, moved, slope, acc, dq, shown, stat, table, sems, out_sem):
    n_pages, p_tok, dim = page_ref.shape
    n_tok = q_ref.shape[1]
    width = BLOCK * n_tok
    per_page = slope_hbm.shape[0] // n_pages
    slots = per_page * BLOCK
    chunk = 64
    parts = range(0, p_tok, chunk)
    scale_in = INV_TEMP * LOG2E
    share = 4
    quarters = p_tok // (share * chunk)

    def fold(x, op):
        x = x.reshape(x.shape[0] // 8, 8, width)
        out = x[0]
        for i in range(1, x.shape[0]):
            out = op(out, x[i])
        return out

    def flip(p, j):
        more = j + 1 < table[p, slots]
        last = p + 1 >= n_pages
        p2 = jnp.where(more, p, jnp.where(last, p, p + 1))
        j2 = jnp.where(more, j + 1, jnp.where(last, j, 0))
        return p2, j2

    def load_block(p, j):
        tie = None
        for k in range(BLOCK):
            rows = q_ref[table[p, j * BLOCK + k]]
            qb[pl.ds(k * n_tok, n_tok), :] = rows
            tie = rows[0:8, :] if tie is None else tie + rows[0:8, :]
        return tie.astype(jnp.float32)

    def similar(p, n, top):
        rows = share * chunk
        tile = page_ref[p, n * rows:(n + 1) * rows, :]
        s = lax.dot_general(tile, qb[...], (((1,), (1,)), ((), ())), preferred_element_type=jnp.float32)
        sim[n * rows:(n + 1) * rows, :] = s
        most = fold(s, jnp.maximum)
        return most if top is None else jnp.maximum(top, most)

    def add_part(p, j, part):
        part = part.T
        for k in range(BLOCK):
            acc[table[p, j * BLOCK + k]] += part[k * n_tok:(k + 1) * n_tok, :]
        return part

    def out_copy(b, slot):
        return pltpu.make_async_copy(slope.at[slot], slope_hbm.at[b], sems.at[slot])

    fetch = pltpu.make_async_copy(table_ref, table, out_sem.at[2])
    fetch.start()
    acc[...] = jnp.zeros_like(acc)
    shown[...] = jnp.zeros_like(shown)
    lane_i = lax.broadcasted_iota(jnp.int32, (width, width), 0) // n_tok
    lane_j = lax.broadcasted_iota(jnp.int32, (width, width), 1) // n_tok
    diag[...] = jnp.where(lane_i == lane_j, 1.0, 0.0).astype(jnp.bfloat16)

    fetch.wait()
    always = table[0, slots] > 0
    load_block(0, 0)
    top = None
    for n in range(quarters):
        top = similar(0, n, top)
    stat[0] = top

    def step(t, carry):
        p0, j0, p, j = carry
        p2, j2 = flip(p, j)
        slot = lax.rem(t, 2)
        b = p * per_page + j

        @pl.when(always)
        def _():
            tie = load_block(p2, j2)
            top = jnp.max(stat[0], axis=0, keepdims=True)
            total = jnp.zeros((8, width), jnp.float32)
            mass = jnp.zeros((8, width), jnp.float32)
            part = None
            for n, i in enumerate(parts):
                if n % share == 0:
                    k = n * chunk
                    term = jnp.dot(page_t_ref[p0, :, k:k + share * chunk], slope[1 - slot, k:k + share * chunk, :],
                                   preferred_element_type=jnp.float32)
                    part = term if part is None else part + term
                r = pl.ds(i, chunk)
                d = (sim[r, :] - top) * scale_in
                e = jnp.exp2(d)
                v = e * d
                wts[r, :] = e
                moved[r, :] = v
                total += fold(e, jnp.add)
                mass += fold(v, jnp.add)
            held[...] = part
            stat[1] = total
            stat[2] = mass
            stat[3] = jnp.broadcast_to(top, (8, width))

        @pl.when(t >= 2)
        def _():
            out_copy(b, slot).wait()

        @pl.when(always)
        def _():
            inv = 1.0 / jnp.sum(stat[1], axis=0, keepdims=True)
            drift = jnp.sum(stat[2], axis=0, keepdims=True) * inv
            matched = stat[3, 0:1, :] + drift * (1.0 / scale_in)
            ahead = 1
            high = None
            for n in range(ahead):
                high = similar(p2, n, high)
            hi = matched.astype(jnp.bfloat16)
            rest = matched - hi.astype(jnp.float32)
            mid = rest.astype(jnp.bfloat16)
            low = (rest - mid.astype(jnp.float32)).astype(jnp.bfloat16)
            pieces = jnp.concatenate([hi, mid, low], axis=0)
            score = jnp.sum(
                jnp.dot(pieces, diag[...], preferred_element_type=jnp.float32), axis=0, keepdims=True)
            place = place_ref[pl.ds(p, 1), :]
            line = shown[pl.ds(p, 1), :]
            for k in range(BLOCK):
                part = score[:, (k * n_tok // LANES) * LANES:(k * n_tok // LANES + 1) * LANES]
                off = k * n_tok % LANES
                if off:
                    part = pltpu.roll(part, LANES - off, 1)
                line = jnp.where(place == j * BLOCK + k, part, line)
            shown[pl.ds(p, 1), :] = line
            scale = (cnt_ref[b] * score - aim_ref[b]) * inv
            beta = scale * (1.0 / LOG2E)
            alpha = scale - beta * drift
            for n, i in enumerate(parts):
                if n % share == 0 and n // share < quarters - ahead:
                    high = similar(p2, ahead + n // share, high)
                r = pl.ds(i, chunk)
                y = alpha * wts[r, :] + beta * moved[r, :]
                slope[slot, r, :] = y.astype(jnp.bfloat16)
            rows = add_part(p0, j0, jnp.where(t >= 1, held[...], 0.0))
            stat[4] = high + y[0:8, :]
            stat[4, :, 0:LANES] = y[0:8, 0:LANES] + rows[0:8, :]
            stat[0] = high

        out_copy(b, slot).start()
        return p, j, p2, j2

    count = table[0, slots]
    for p in range(1, n_pages):
        count += table[p, slots]
    zero = jnp.int32(0)
    p, j, _, _ = lax.fori_loop(0, count, step, (zero, zero, zero, zero))
    add_part(p, j, jnp.dot(page_t_ref[p], slope[lax.rem(count - 1, 2)], preferred_element_type=jnp.float32))
    dq[...] = acc[...].astype(dq.dtype)
    dq_copy = pltpu.make_async_copy(dq, dq_hbm, out_sem.at[0])
    score_copy = pltpu.make_async_copy(shown, score_hbm, out_sem.at[1])
    dq_copy.start()
    score_copy.start()
    out_copy(0, 0).wait()
    out_copy(0, 1).wait()
    dq_copy.wait()
    score_copy.wait()


def page_kernel(table, q_ref, slope_hbm, out_hbm, qb, buf, out, sems, out_sems):
    n_pages, p_tok, dim = out_hbm.shape
    n_tok = q_ref.shape[1]
    width = BLOCK * n_tok
    per_page = slope_hbm.shape[0] // n_pages
    slots = per_page * BLOCK

    def fetch(b):
        return pltpu.make_async_copy(slope_hbm.at[b], buf.at[b], sems.at[b])

    def store(p, slot):
        return pltpu.make_async_copy(out.at[slot], out_hbm.at[p], out_sems.at[slot])

    for p in range(n_pages):
        for j in range(per_page):
            @pl.when(j < table[p, slots])
            def _():
                fetch(p * per_page + j).start()

    def page_step(p, c):
        slot = lax.rem(p, 2)
        number = table[p, slots]

        @pl.when(p >= 2)
        def _():
            store(p, slot).wait()
        for n in range(1, per_page + 1):
            @pl.when(number == n)
            def _():
                total = None
                for k in range(n * BLOCK):
                    qb[pl.ds(k * n_tok, n_tok), :] = q_ref[table[p, k]]
                for j in range(n):
                    fetch(p * per_page + j).wait()
                for j in range(n):
                    term = jnp.dot(buf[p * per_page + j], qb[pl.ds(j * width, width), :],
                                   preferred_element_type=jnp.float32)
                    total = term if total is None else total + term
                out[slot] = total.astype(out.dtype)
        store(p, slot).start()
        return c
    lax.fori_loop(0, n_pages, page_step, 0)
    for p in range(max(n_pages - 2, 0), n_pages):
        store(p, p % 2).wait()


def body(queries, pages, users, page_count, teacher):
    n_dev = lax.axis_size("group") * lax.axis_size("member")
    own, n_tok, dim = queries.shape
    n_pages, p_tok, _ = pages.shape
    slots = users.shape[1]
    n_query = n_dev * own
    per_page = slots // BLOCK
    n_blocks = n_pages * per_page
    width = BLOCK * n_tok
    smem = pl.BlockSpec(memory_space=pltpu.SMEM)
    vmem = pl.BlockSpec(memory_space=pltpu.VMEM)
    hbm = pl.BlockSpec(memory_space=pltpu.HBM)

    copies = jnp.broadcast_to(queries[None], (n_dev, own, n_tok, dim))
    copies = lax.optimization_barrier(copies)
    gathered = lax.all_to_all(copies, AXES, split_axis=0, concat_axis=0, tiled=True)
    gathered = gathered.reshape(n_query, n_tok, dim)
    page_t = jnp.swapaxes(pages, 1, 2)

    table, place, cnt, aim = pl.pallas_call(
        plan_kernel,
        out_shape=(
            jax.ShapeDtypeStruct((n_pages, LANES), jnp.int32),
            jax.ShapeDtypeStruct((n_pages, LANES), jnp.int32),
            jax.ShapeDtypeStruct((n_blocks, 1, width), jnp.float32),
            jax.ShapeDtypeStruct((n_blocks, 1, width), jnp.float32),
        ),
        in_specs=[smem, vmem, vmem],
        out_specs=(vmem,) * 4,
        compiler_params=pltpu.CompilerParams(vmem_limit_bytes=16 << 20),
        cost_estimate=pl.CostEstimate(flops=10**6, bytes_accessed=1 << 16, transcendentals=0),
        name="plan",
    )(page_count, users, teacher)

    dq, slope, scores = pl.pallas_call(
        grad_kernel,
        out_shape=(
            jax.ShapeDtypeStruct((n_query, n_tok, dim), jnp.bfloat16),
            jax.ShapeDtypeStruct((n_blocks, p_tok, width), jnp.bfloat16),
            jax.ShapeDtypeStruct((n_pages, LANES), jnp.float32),
        ),
        in_specs=[vmem] * 7 + [hbm],
        out_specs=(hbm, hbm, hbm),
        input_output_aliases={7: 0},
        scratch_shapes=[
            pltpu.VMEM((width, dim), jnp.bfloat16),
            pltpu.VMEM((width, width), jnp.bfloat16),
            pltpu.VMEM((dim, width), jnp.float32),
            pltpu.VMEM((p_tok, width), jnp.float32),
            pltpu.VMEM((p_tok, width), jnp.float32),
            pltpu.VMEM((p_tok, width), jnp.float32),
            pltpu.VMEM((2, p_tok, width), jnp.bfloat16),
            pltpu.VMEM((n_query, n_tok, dim), jnp.float32),
            pltpu.VMEM((n_query, n_tok, dim), jnp.bfloat16),
            pltpu.VMEM((n_pages, LANES), jnp.float32),
            pltpu.VMEM((6, 8, width), jnp.float32),
            pltpu.SMEM((n_pages, LANES), jnp.int32),
            pltpu.SemaphoreType.DMA((2,)),
            pltpu.SemaphoreType.DMA((3,)),
        ],
        compiler_params=pltpu.CompilerParams(vmem_limit_bytes=48 << 20),
        cost_estimate=pl.CostEstimate(flops=4 * 10**9, bytes_accessed=16 << 20, transcendentals=4 << 20),
        name="grad",
    )(table, gathered, pages, page_t, cnt, aim, place, copies.reshape(n_query, n_tok, dim))

    terms = lax.all_to_all(
        dq.reshape(n_dev, own, n_tok, dim), AXES, split_axis=0, concat_axis=0, tiled=True)

    page_grad = pl.pallas_call(
        page_kernel,
        out_shape=jax.ShapeDtypeStruct(pages.shape, pages.dtype),
        in_specs=[smem, vmem, hbm],
        out_specs=hbm,
        scratch_shapes=[
            pltpu.VMEM((slots * n_tok, dim), jnp.bfloat16),
            pltpu.VMEM((n_blocks, p_tok, width), jnp.bfloat16),
            pltpu.VMEM((2, p_tok, dim), jnp.bfloat16),
            pltpu.SemaphoreType.DMA((n_blocks,)),
            pltpu.SemaphoreType.DMA((2,)),
        ],
        compiler_params=pltpu.CompilerParams(vmem_limit_bytes=48 << 20),
        cost_estimate=pl.CostEstimate(flops=2 * 10**9, bytes_accessed=16 << 20, transcendentals=0),
        name="page_part",
    )(table, gathered, slope)

    query_grad = jnp.sum(terms.astype(jnp.float32), axis=0)
    return scores[:, :slots], query_grad, page_grad


def solution(mesh):
    return jax.shard_map(
        body,
        mesh=mesh,
        in_specs=(P(AXES, None, None), P(AXES, None, None), P(AXES, None), P(AXES), P(AXES, None)),
        out_specs=(P(AXES, None), P(AXES, None, None), P(AXES, None, None)),
        check_vma=False,
    )
```

```python
import jax
import jax.numpy as jnp
from jax import lax
from jax.experimental import pallas as pl
from jax.experimental.pallas import tpu as pltpu
from jax.sharding import PartitionSpec as P

AXES = ("group", "member")
BLOCK = 8
LANES = 128
INV_TEMP = 20.0
LOG2E = 1.4426950408889634


def plan_kernel(count, users_ref, teacher_ref, table_ref, place_ref, cnt_ref, aim_ref):
    n_pages, slots = users_ref.shape
    width = cnt_ref.shape[2]
    per_page = cnt_ref.shape[0] // n_pages
    n_tok = width // BLOCK
    square = (LANES, LANES)
    pad = jnp.zeros((LANES - n_pages, slots), jnp.float32)
    side = jnp.zeros((LANES, LANES - slots), jnp.float32)
    wide = jnp.concatenate(
        [jnp.concatenate([users_ref[...].astype(jnp.float32), pad], axis=0), side], axis=1)
    tall = wide.T
    row = lax.broadcasted_iota(jnp.int32, (slots, LANES), 0)
    col = lax.broadcasted_iota(jnp.int32, (slots, LANES), 1)
    colf = col.astype(jnp.float32)
    teach = jnp.concatenate([teacher_ref[...], jnp.zeros((n_pages, LANES - slots), jnp.float32)], axis=1)
    spread_k = lax.broadcasted_iota(jnp.int32, (slots, slots * n_tok), 0)
    spread_l = lax.broadcasted_iota(jnp.int32, (slots, slots * n_tok), 1)
    spread = jnp.where((spread_l >= spread_k * n_tok) & (spread_l < (spread_k + 1) * n_tok), 1.0, 0.0)
    for p in range(n_pages):
        total = count[p]
        ucol = tall[0:slots, p:p + 1]
        urow = wide[p:p + 1, :]
        alive = (row < total) & (col < total)
        same = jnp.where((ucol == urow) & alive, 1.0, 0.0)
        before_c = jnp.sum(jnp.where(col < row, same, 0.0), axis=1, keepdims=True)
        before_r = jnp.sum(jnp.where(row < col, same, 0.0), axis=0, keepdims=True)
        first_c = (before_c == 0.0) & (row[:, 0:1] < total)
        first_r = (before_r == 0.0) & (col[0:1, :] < total)
        first_cf = jnp.where(first_c, 1.0, 0.0)
        first_rf = jnp.where(first_r, 1.0, 0.0)
        rank_c = jnp.sum(jnp.where(col < row, first_rf, 0.0), axis=1, keepdims=True)
        number = jnp.sum(first_rf, axis=1, keepdims=True)
        put = jnp.where(rank_c == colf, first_cf, 0.0)
        order = jnp.sum(put * ucol, axis=0, keepdims=True)
        hits = jnp.sum(same, axis=1, keepdims=True)
        aims = jnp.sum(same * teach[p:p + 1, :], axis=1, keepdims=True)
        cnt = jnp.sum(put * hits, axis=0, keepdims=True)
        aim = jnp.sum(put * aims, axis=0, keepdims=True)
        place = jnp.sum(same * (first_cf * rank_c), axis=0, keepdims=True)
        blocks = jnp.floor((number + (BLOCK - 1)) * (1.0 / BLOCK))
        entry = jnp.where(col[0:1, :] == slots, blocks, order)
        table_ref[p:p + 1, :] = entry.astype(jnp.int32)
        place_ref[p:p + 1, :] = jnp.where(col[0:1, :] < total, place, -1.0).astype(jnp.int32)
        both = jnp.concatenate([cnt, aim, jnp.zeros((6, LANES), jnp.float32)], axis=0)[:, 0:slots]
        lanes = jnp.dot(both, spread, precision=lax.Precision.HIGHEST,
                        preferred_element_type=jnp.float32)
        for j in range(per_page):
            cnt_ref[p * per_page + j] = lanes[0:1, j * width:(j + 1) * width]
            aim_ref[p * per_page + j] = lanes[1:2, j * width:(j + 1) * width]


def grad_kernel(table_ref, q_ref, page_ref, page_t_ref, cnt_ref, aim_ref, place_ref, spent_hbm,
                dq_hbm, slope_hbm, score_hbm,
                qb, diag, held, sim, wts, moved, slope, acc, dq, shown, stat, table, sems, out_sem, dq_sems):
    n_pages, p_tok, dim = page_ref.shape
    n_tok = q_ref.shape[1]
    width = BLOCK * n_tok
    per_page = slope_hbm.shape[0] // n_pages
    slots = per_page * BLOCK
    chunk = 64
    parts = range(0, p_tok, chunk)
    scale_in = INV_TEMP * LOG2E
    share = 4
    quarters = p_tok // (share * chunk)

    def fold(x, op):
        x = x.reshape(x.shape[0] // 8, 8, width)
        out = x[0]
        for i in range(1, x.shape[0]):
            out = op(out, x[i])
        return out

    def flip(p, j):
        more = j + 1 < table[p, slots]
        last = p + 1 >= n_pages
        p2 = jnp.where(more, p, jnp.where(last, p, p + 1))
        j2 = jnp.where(more, j + 1, jnp.where(last, j, 0))
        return p2, j2

    def load_block(p, j):
        tie = None
        for k in range(BLOCK):
            rows = q_ref[table[p, j * BLOCK + k]]
            qb[pl.ds(k * n_tok, n_tok), :] = rows
            tie = rows[0:8, :] if tie is None else tie + rows[0:8, :]
        return tie.astype(jnp.float32)

    def similar(p, n, top):
        rows = share * chunk
        tile = page_ref[p, n * rows:(n + 1) * rows, :]
        s = lax.dot_general(tile, qb[...], (((1,), (1,)), ((), ())), preferred_element_type=jnp.float32)
        sim[n * rows:(n + 1) * rows, :] = s
        most = fold(s, jnp.maximum)
        return most if top is None else jnp.maximum(top, most)

    def add_part(p, j, part):
        part = part.T
        for k in range(BLOCK):
            acc[table[p, j * BLOCK + k]] += part[k * n_tok:(k + 1) * n_tok, :]
        return part

    def out_copy(b, slot):
        return pltpu.make_async_copy(slope.at[slot], slope_hbm.at[b], sems.at[slot])

    fetch = pltpu.make_async_copy(table_ref, table, out_sem.at[2])
    fetch.start()
    acc[...] = jnp.zeros_like(acc)
    shown[...] = jnp.zeros_like(shown)
    lane_i = lax.broadcasted_iota(jnp.int32, (width, width), 0) // n_tok
    lane_j = lax.broadcasted_iota(jnp.int32, (width, width), 1) // n_tok
    diag[...] = jnp.where(lane_i == lane_j, 1.0, 0.0).astype(jnp.bfloat16)

    fetch.wait()
    always = table[0, slots] > 0
    load_block(0, 0)
    top = None
    for n in range(quarters):
        top = similar(0, n, top)
    stat[0] = top

    def step(t, carry):
        p0, j0, p, j = carry
        p2, j2 = flip(p, j)
        slot = lax.rem(t, 2)
        b = p * per_page + j

        @pl.when(always)
        def _():
            tie = load_block(p2, j2)
            top = jnp.max(stat[0], axis=0, keepdims=True)
            total = jnp.zeros((8, width), jnp.float32)
            mass = jnp.zeros((8, width), jnp.float32)
            part = None
            for n, i in enumerate(parts):
                if n % share == 0:
                    k = n * chunk
                    term = jnp.dot(page_t_ref[p0, :, k:k + share * chunk], slope[1 - slot, k:k + share * chunk, :],
                                   preferred_element_type=jnp.float32)
                    part = term if part is None else part + term
                r = pl.ds(i, chunk)
                d = (sim[r, :] - top) * scale_in
                e = jnp.exp2(d)
                v = e * d
                wts[r, :] = e
                moved[r, :] = v
                total += fold(e, jnp.add)
                mass += fold(v, jnp.add)
            held[...] = part
            stat[1] = total
            stat[2] = mass
            stat[3] = jnp.broadcast_to(top, (8, width))

        @pl.when(t >= 2)
        def _():
            out_copy(b, slot).wait()

        @pl.when(always)
        def _():
            inv = 1.0 / jnp.sum(stat[1], axis=0, keepdims=True)
            drift = jnp.sum(stat[2], axis=0, keepdims=True) * inv
            matched = stat[3, 0:1, :] + drift * (1.0 / scale_in)
            ahead = 1
            high = None
            for n in range(ahead):
                high = similar(p2, n, high)
            hi = matched.astype(jnp.bfloat16)
            rest = matched - hi.astype(jnp.float32)
            mid = rest.astype(jnp.bfloat16)
            low = (rest - mid.astype(jnp.float32)).astype(jnp.bfloat16)
            pieces = jnp.concatenate([hi, mid, low], axis=0)
            score = jnp.sum(
                jnp.dot(pieces, diag[...], preferred_element_type=jnp.float32), axis=0, keepdims=True)
            place = place_ref[pl.ds(p, 1), :]
            line = shown[pl.ds(p, 1), :]
            for k in range(BLOCK):
                part = score[:, (k * n_tok // LANES) * LANES:(k * n_tok // LANES + 1) * LANES]
                off = k * n_tok % LANES
                if off:
                    part = pltpu.roll(part, LANES - off, 1)
                line = jnp.where(place == j * BLOCK + k, part, line)
            shown[pl.ds(p, 1), :] = line
            scale = (cnt_ref[b] * score - aim_ref[b]) * inv
            beta = scale * (1.0 / LOG2E)
            alpha = scale - beta * drift
            for n, i in enumerate(parts):
                if n % share == 0 and n // share < quarters - ahead:
                    high = similar(p2, ahead + n // share, high)
                r = pl.ds(i, chunk)
                y = alpha * wts[r, :] + beta * moved[r, :]
                slope[slot, r, :] = y.astype(jnp.bfloat16)
            rows = add_part(p0, j0, jnp.where(t >= 1, held[...], 0.0))
            stat[4] = high + y[0:8, :]
            stat[4, :, 0:LANES] = y[0:8, 0:LANES] + rows[0:8, :]
            stat[0] = high

        out_copy(b, slot).start()
        return p, j, p2, j2

    count = table[0, slots]
    for p in range(1, n_pages):
        count += table[p, slots]
    zero = jnp.int32(0)
    p, j, _, _ = lax.fori_loop(0, count, step, (zero, zero, zero, zero))
    score_copy = pltpu.make_async_copy(shown, score_hbm, out_sem.at[0])
    score_copy.start()
    add_part(p, j, jnp.dot(page_t_ref[p], slope[lax.rem(count - 1, 2)], preferred_element_type=jnp.float32))
    moves = []
    for n, k in enumerate(range(0, q_ref.shape[0], BLOCK)):
        rows = pl.ds(k, BLOCK)
        dq[rows] = acc[rows].astype(dq.dtype)
        move = pltpu.make_async_copy(dq.at[rows], dq_hbm.at[rows], dq_sems.at[n])
        move.start()
        moves.append(move)
    out_copy(0, 0).wait()
    out_copy(0, 1).wait()
    score_copy.wait()
    for move in moves:
        move.wait()


def page_kernel(table, q_ref, slope_hbm, out_hbm, qb, buf, out, sems, out_sems):
    n_pages, p_tok, dim = out_hbm.shape
    n_tok = q_ref.shape[1]
    width = BLOCK * n_tok
    per_page = slope_hbm.shape[0] // n_pages
    slots = per_page * BLOCK

    def fetch(b):
        return pltpu.make_async_copy(slope_hbm.at[b], buf.at[b], sems.at[b])

    def store(p, slot):
        return pltpu.make_async_copy(out.at[slot], out_hbm.at[p], out_sems.at[slot])

    for p in range(n_pages):
        for j in range(per_page):
            @pl.when(j < table[p, slots])
            def _():
                fetch(p * per_page + j).start()

    def page_step(p, c):
        slot = lax.rem(p, 2)
        number = table[p, slots]

        @pl.when(p >= 2)
        def _():
            store(p, slot).wait()
        for n in range(1, per_page + 1):
            @pl.when(number == n)
            def _():
                total = None
                for k in range(n * BLOCK):
                    qb[pl.ds(k * n_tok, n_tok), :] = q_ref[table[p, k]]
                for j in range(n):
                    fetch(p * per_page + j).wait()
                for j in range(n):
                    term = jnp.dot(buf[p * per_page + j], qb[pl.ds(j * width, width), :],
                                   preferred_element_type=jnp.float32)
                    total = term if total is None else total + term
                out[slot] = total.astype(out.dtype)
        store(p, slot).start()
        return c
    lax.fori_loop(0, n_pages, page_step, 0)
    for p in range(max(n_pages - 2, 0), n_pages):
        store(p, p % 2).wait()


def body(queries, pages, users, page_count, teacher):
    n_dev = lax.axis_size("group") * lax.axis_size("member")
    own, n_tok, dim = queries.shape
    n_pages, p_tok, _ = pages.shape
    slots = users.shape[1]
    n_query = n_dev * own
    per_page = slots // BLOCK
    n_blocks = n_pages * per_page
    width = BLOCK * n_tok
    smem = pl.BlockSpec(memory_space=pltpu.SMEM)
    vmem = pl.BlockSpec(memory_space=pltpu.VMEM)
    hbm = pl.BlockSpec(memory_space=pltpu.HBM)

    copies = jnp.broadcast_to(queries[None], (n_dev, own, n_tok, dim))
    copies = lax.optimization_barrier(copies)
    gathered = lax.all_to_all(copies, AXES, split_axis=0, concat_axis=0, tiled=True)
    gathered = gathered.reshape(n_query, n_tok, dim)
    page_t = jnp.swapaxes(pages, 1, 2)

    table, place, cnt, aim = pl.pallas_call(
        plan_kernel,
        out_shape=(
            jax.ShapeDtypeStruct((n_pages, LANES), jnp.int32),
            jax.ShapeDtypeStruct((n_pages, LANES), jnp.int32),
            jax.ShapeDtypeStruct((n_blocks, 1, width), jnp.float32),
            jax.ShapeDtypeStruct((n_blocks, 1, width), jnp.float32),
        ),
        in_specs=[smem, vmem, vmem],
        out_specs=(vmem,) * 4,
        compiler_params=pltpu.CompilerParams(vmem_limit_bytes=16 << 20),
        cost_estimate=pl.CostEstimate(flops=10**6, bytes_accessed=1 << 16, transcendentals=0),
        name="plan",
    )(page_count, users, teacher)

    dq, slope, scores = pl.pallas_call(
        grad_kernel,
        out_shape=(
            jax.ShapeDtypeStruct((n_query, n_tok, dim), jnp.bfloat16),
            jax.ShapeDtypeStruct((n_blocks, p_tok, width), jnp.bfloat16),
            jax.ShapeDtypeStruct((n_pages, LANES), jnp.float32),
        ),
        in_specs=[vmem] * 7 + [hbm],
        out_specs=(hbm, hbm, hbm),
        input_output_aliases={7: 0},
        scratch_shapes=[
            pltpu.VMEM((width, dim), jnp.bfloat16),
            pltpu.VMEM((width, width), jnp.bfloat16),
            pltpu.VMEM((dim, width), jnp.float32),
            pltpu.VMEM((p_tok, width), jnp.float32),
            pltpu.VMEM((p_tok, width), jnp.float32),
            pltpu.VMEM((p_tok, width), jnp.float32),
            pltpu.VMEM((2, p_tok, width), jnp.bfloat16),
            pltpu.VMEM((n_query, n_tok, dim), jnp.float32),
            pltpu.VMEM((n_query, n_tok, dim), jnp.bfloat16),
            pltpu.VMEM((n_pages, LANES), jnp.float32),
            pltpu.VMEM((6, 8, width), jnp.float32),
            pltpu.SMEM((n_pages, LANES), jnp.int32),
            pltpu.SemaphoreType.DMA((2,)),
            pltpu.SemaphoreType.DMA((3,)),
            pltpu.SemaphoreType.DMA((n_query // BLOCK,)),
        ],
        compiler_params=pltpu.CompilerParams(vmem_limit_bytes=48 << 20),
        cost_estimate=pl.CostEstimate(flops=4 * 10**9, bytes_accessed=16 << 20, transcendentals=4 << 20),
        name="grad",
    )(table, gathered, pages, page_t, cnt, aim, place, copies.reshape(n_query, n_tok, dim))

    terms = lax.all_to_all(
        dq.reshape(n_dev, own, n_tok, dim), AXES, split_axis=0, concat_axis=0, tiled=True)

    page_grad = pl.pallas_call(
        page_kernel,
        out_shape=jax.ShapeDtypeStruct(pages.shape, pages.dtype),
        in_specs=[smem, vmem, hbm],
        out_specs=hbm,
        scratch_shapes=[
            pltpu.VMEM((slots * n_tok, dim), jnp.bfloat16),
            pltpu.VMEM((n_blocks, p_tok, width), jnp.bfloat16),
            pltpu.VMEM((2, p_tok, dim), jnp.bfloat16),
            pltpu.SemaphoreType.DMA((n_blocks,)),
            pltpu.SemaphoreType.DMA((2,)),
        ],
        compiler_params=pltpu.CompilerParams(vmem_limit_bytes=48 << 20),
        cost_estimate=pl.CostEstimate(flops=2 * 10**9, bytes_accessed=16 << 20, transcendentals=0),
        name="page_part",
    )(table, gathered, slope)

    query_grad = jnp.sum(terms.astype(jnp.float32), axis=0)
    return scores[:, :slots], query_grad, page_grad


def solution(mesh):
    return jax.shard_map(
        body,
        mesh=mesh,
        in_specs=(P(AXES, None, None), P(AXES, None, None), P(AXES, None), P(AXES), P(AXES, None)),
        out_specs=(P(AXES, None), P(AXES, None, None), P(AXES, None, None)),
        check_vma=False,
    )
```
